128 devices in a mesh: dp: 16 (over z, y_hi, core), tensor: 8 (over x, y_lo).
Axes of the slice: x: 4, y: 4 (y_hi: 2, y_lo: 2; y = y_hi * 2 + y_lo), z: 4, core: 2. Of those that a mesh axis runs over, the one named last changes fastest.
Arguments:
- train_states: bfloat16 [4096, 8192], P('dp'), may hold values from -6 to 6
- qkv_cotangent: bfloat16 [4096, 6144], P('dp', 'tensor'), may hold values from -0.09375 to 0.09375
- w_master: float32 [8192, 6144], P('dp', 'tensor'), may hold values from -1.1048543 to 1.1048543
- moment_one: float32 [8192, 6144], P('dp', 'tensor'), may hold values from -1.8 to 1.8
- moment_two: float32 [8192, 6144], P('dp', 'tensor'), may hold values from 0.02 to 2
- prompt_states: bfloat16 [8192, 8192], P('dp'), may hold values from -45 to 45
- norm_gain: float32 [8192], replicated, may hold values from 0.1 to 1.9
- w_out: bfloat16 [4096, 8192], P('tensor'), may hold values from -0.09375 to 0.09375
Outputs:
- update_dir: float32 [8192, 6144], P('dp', 'tensor')
- prefill_out: bfloat16 [8192, 8192], P(('dp', 'tensor'))
The draws below stay inside these ranges and needn't reach their ends.
All inputs are finite; a program needn't handle non-finite values.
Results may differ from the reference program's by a relative error of at most 0.02.
Values may be sent and summed in bfloat16 or wider, within the bound.
A program may use at most 128 MiB of HBM per device.

```python
import math
import jax
import jax.numpy as jnp
from jax import lax

D = 8192
HD = 128
QH_DEV = 4
KV_DEV = 1
TRG = 256
LEN = 512
HEADS = 32
QKV_COLS = 6144
TRAIN = 4096
N_DP = 16
N_TENSOR = 8


def draw_prompt_states(key, part):
    row_total = LEN * N_DP
    key_values, key_scales, key_columns = jax.random.split(key, 3)
    spread = 0.5 * math.log(10.0)
    values_draw = jax.random.truncated_normal(key_values, -4.0, 4.0, (row_total, D), jnp.float32)
    row_scale = jnp.exp(jax.random.uniform(key_scales, (row_total, 1), jnp.float32, -spread, spread))
    column_scale = jnp.exp(jax.random.uniform(key_columns, (1, D), jnp.float32, -spread, spread))
    return (values_draw * row_scale * column_scale).astype(jnp.bfloat16)


def draw_w_master(key, part):
    slice_width = (QH_DEV + 2 * KV_DEV) * HD
    key_base = jax.random.fold_in(key, 0)
    base_draw = jax.random.truncated_normal(key_base, -4.0, 4.0, (D, N_TENSOR, slice_width), jnp.float32) / math.sqrt(D)
    return base_draw.reshape(D, N_TENSOR * slice_width)


def spiked(entries, key, source, target, parts, factor):
    def block_of(axis_at):
        return (jnp.arange(entries.shape[axis_at]) // (entries.shape[axis_at] // parts)).reshape((-1,) + (1,) * (entries.ndim - 1 - axis_at))

    first = jax.random.permutation(key, parts)[block_of(target)]
    other_side = (block_of(target) + parts // 2) % parts
    return jnp.where((block_of(source) == first) | (block_of(source) == other_side), factor * entries, entries)


def shard_levels(stream_key, shape, cuts, low, largest):
    gain = 1.0
    for dim, parts in cuts:
        steps = jax.random.uniform(jax.random.fold_in(jax.random.fold_in(stream_key, 6), dim), (parts,), jnp.float32, low / len(cuts), largest / len(cuts))
        gain = gain * jnp.repeat(jnp.exp(steps), shape[dim] // parts).reshape((-1,) + (1,) * (len(shape) - 1 - dim))
    return gain


def scatter_about(rng, extent, width, reach, cuts=(), held_as=jnp.bfloat16):
    drawn = width * jax.random.normal(rng, extent, jnp.float32)
    if cuts:
        drawn = drawn * shard_levels(rng, extent, cuts, -0.22, 0.18)
    return jnp.clip(drawn, -reach, reach).astype(held_as)


def gaussian_with(own_key, extent, deviation, reach, shards, heavy, held_as=jnp.bfloat16):
    drawn = deviation * jax.random.normal(own_key, extent, jnp.float32)
    if shards:
        drawn = drawn * shard_levels(own_key, extent, shards, -0.22, 0.18)
    return jnp.clip(spiked(drawn, jax.random.fold_in(own_key, 3), *heavy), -reach, reach).astype(held_as)


def setup_inputs(seed: int = 0) -> dict:
    arg_keys = jax.random.split(jax.random.key(seed), 9)
    return {
        "train_states": gaussian_with(arg_keys[0], (TRAIN, D), 1.0, 6.0, ((0, 16),), (0, 1, 16, 2.0)),
        "qkv_cotangent": scatter_about(arg_keys[1], (TRAIN, QKV_COLS), (1.0 / (TRG * N_DP) ** 0.5), 0.09375, ((0, 16), (1, 8))),
        "w_master": draw_w_master(jax.random.fold_in(arg_keys[8], 71), 0),
        "moment_one": scatter_about(arg_keys[3], (D, QKV_COLS), 0.3, 1.8, ((0, 16), (1, 8)), jnp.float32),
        "moment_two": jnp.clip(jnp.exp(math.log(2.0) - 4.6051702 * jax.random.uniform(arg_keys[4], (D, QKV_COLS), jnp.float32) ** shard_levels(arg_keys[4], (D, QKV_COLS), ((0, 16), (1, 8)), -0.2, 0.2)), 0.02, 2.0),
        "prompt_states": draw_prompt_states(jax.random.fold_in(arg_keys[8], 71), 0),
        "norm_gain": jnp.clip(1.0 + 0.18 * jax.random.normal(arg_keys[6], (D,), jnp.float32), 0.1, 1.9),
        "w_out": scatter_about(arg_keys[7], (HEADS * HD, D), (HEADS * HD) ** -0.5, 0.09375, ((0, 8),)),
    }


beta_one = 0.9
beta_two = 0.95
bias_one = 1.0 - 0.9 ** 8
bias_two = 1.0 - 0.95 ** 8
learn_rate = 0.002
adam_eps = 1e-08
norm_eps = 1e-05
rope_base = 500000.0

def rope_tables(length, head_size):
    half_width = head_size // 2
    exponent = jnp.arange(half_width, dtype=jnp.float32) * (2.0 / head_size)
    inverse = jnp.power(jnp.float32(rope_base), -exponent)
    position = jnp.arange(length, dtype=jnp.float32)
    angles = position[:, None] * inverse[None, :]
    cosine_table = jnp.concatenate([jnp.cos(angles), jnp.cos(angles)], axis=1)
    sine_table = jnp.concatenate([jnp.sin(angles), jnp.sin(angles)], axis=1)
    return (cosine_table, sine_table)

def rotate(head_block, cosine_table, sine_table):
    half_width = head_block.shape[-1] // 2
    turned = jnp.concatenate([-head_block[..., half_width:], head_block[..., :half_width]], axis=-1)
    return head_block * cosine_table + turned * sine_table

def reference(train_states, qkv_cotangent, w_master, moment_one, moment_two, prompt_states, norm_gain, w_out):
    gradient = jnp.dot(train_states.T, qkv_cotangent, preferred_element_type=jnp.float32)
    moment_new = beta_one * moment_one + (1.0 - beta_one) * gradient
    second_new = beta_two * moment_two + (1.0 - beta_two) * gradient * gradient
    update_dir = moment_new / bias_one / (jnp.sqrt(second_new / bias_two) + adam_eps)
    qkv_weight = (w_master - learn_rate * update_dir).astype(jnp.bfloat16)
    slice_width = (QH_DEV + 2 * KV_DEV) * HD
    query_width = QH_DEV * HD
    score_scale = HD ** (-0.5)
    cosine_table, sine_table = rope_tables(LEN, HD)
    causal = jnp.arange(LEN)[:, None] >= jnp.arange(LEN)[None, :]
    out_blocks = w_out.reshape(N_TENSOR, query_width, D).astype(jnp.float32)

    def prefill_group(states):
        widened = states.astype(jnp.float32)
        mean_square = lax.optimization_barrier(jnp.mean(widened * widened, axis=1, keepdims=True))
        normed = (widened * lax.rsqrt(mean_square + norm_eps) * norm_gain).astype(jnp.bfloat16)
        projected = jnp.dot(normed, qkv_weight, preferred_element_type=jnp.float32)
        projected = projected.reshape(LEN, N_TENSOR, slice_width)
        queries = projected[:, :, :query_width].reshape(LEN, N_TENSOR, QH_DEV, HD)
        queries = (rotate(queries, cosine_table[:, None, None, :], sine_table[:, None, None, :]) * score_scale).astype(jnp.bfloat16)
        key_rows = rotate(projected[:, :, query_width:query_width + HD], cosine_table[:, None, :], sine_table[:, None, :]).astype(jnp.bfloat16)
        value_rows = projected[:, :, query_width + HD:].astype(jnp.bfloat16)
        scores = jnp.einsum('qjhd,kjd->jhqk', queries.astype(jnp.float32), key_rows.astype(jnp.float32))
        scores = jnp.where(causal[None, None], scores, -jnp.inf)
        attend_weights = jax.nn.softmax(scores, axis=-1).astype(jnp.bfloat16)
        attended = jnp.einsum('jhqk,kjd->qjhd', attend_weights.astype(jnp.float32), value_rows.astype(jnp.float32)).astype(jnp.bfloat16)
        attended = attended.reshape(LEN, N_TENSOR, query_width)
        head_part = jnp.einsum('qja,jad->jqd', attended.astype(jnp.float32), out_blocks).astype(jnp.bfloat16)
        head_part = lax.optimization_barrier(head_part)
        return lax.optimization_barrier(jnp.sum(head_part.astype(jnp.float32), axis=0)).astype(jnp.bfloat16)
    outputs = lax.map(prefill_group, prompt_states.reshape(N_DP, LEN, D))
    return (update_dir, outputs.reshape(N_DP * LEN, D))
```

```python
import functools

import jax
import jax.numpy as jnp
import numpy as np
from jax import lax
from jax.experimental import pallas as pl
from jax.experimental.pallas import tpu as pltpu
from jax.sharding import PartitionSpec as P

HD = 128
QH = 4
LEN = 512
D = 8192
N_DP = 16
N_T = 8
SLICE = (QH + 2) * HD
QW = QH * HD
ROWS = D // N_DP
TOK = 256
SUB = TOK // N_T
HALF = D // 2
CHUNKS = 4
CW = HALF // CHUNKS

beta_one = 0.9
beta_two = 0.95
bias_one = 1.0 - 0.9**8
bias_two = 1.0 - 0.95**8
learn_rate = 0.002
adam_eps = 1e-08
norm_eps = 1e-05
rope_base = 500000.0

MESH = pl.DeviceIdType.MESH
BF = jnp.bfloat16
F32 = jnp.float32


def place():
    d = lax.axis_index("dp")
    t = lax.axis_index("tensor")
    return d, t, d // 4, (d // 2) % 2, d % 2, t // 2, t % 2


def mo(v, m):
    return pl.multiple_of(v, m)


def greet(peers):
    barrier = pltpu.get_barrier_semaphore()
    for peer in peers:
        pl.semaphore_signal(barrier, inc=1, device_id=peer, device_id_type=MESH)
    pl.semaphore_wait(barrier, len(peers))


class Copies:
    def __init__(self, send, recv):
        self.send, self.recv, self.made, self.used = send, recv, {}, 0

    def start(self, name, src, dst, peer):
        cp = pltpu.make_async_remote_copy(
            src_ref=src,
            dst_ref=dst,
            send_sem=self.send.at[self.used],
            recv_sem=self.recv.at[self.used],
            device_id=peer,
            device_id_type=MESH,
        )
        self.used += 1
        self.made[name] = cp
        cp.start()

    def arrived(self, *names):
        for name in names:
            self.made[name].wait_recv()

    def drain(self):
        for cp in self.made.values():
            cp.wait_send()


class Gather:
    def __init__(self, tag, cps, buf, index, rows, cross, nxt, prv, partner, core=None):
        self.tag, self.cps, self.buf, self.index = tag, cps, buf, index
        self.rows, self.cross = rows, cross
        self.nxt, self.prv, self.partner, self.core = nxt, prv, partner, core

    def piece(self, rr, plane, lo, hi):
        return self.buf.at[self.index(rr, plane), pl.ds(lo, hi - lo), :]

    def go(self, name, rr, plane, lo, hi, peer, src=None):
        dst = self.piece(rr, plane, lo, hi)
        if src is None:
            src = dst
        self.cps.start(self.tag + name, src, dst, peer)

    def wait(self, *names):
        self.cps.arrived(*[self.tag + name for name in names])

    def begin(self, own=None):
        rows, cross = self.rows, self.cross
        half, ch = rows // 2, self.cross // 2

        def src(lo, hi):
            if own is None:
                return None
            return own.at[pl.ds(lo, hi - lo), :]

        def send(name, lo, hi, peer):
            self.go(name, 0, 0, lo, hi, peer, src(lo, hi))

        send("oA+", 0, half, self.nxt)
        send("oB-", half, rows, self.prv)
        send("oPA", 0, ch, self.partner)
        send("oPB", ch, cross, self.partner)
        send("oB+", half, rows, self.nxt)
        send("oA-", 0, half, self.prv)
        if cross < rows:
            send("oP2", cross, rows, self.partner)
        if self.core is not None:
            send("c00", 0, rows, self.core)

    def step1(self):
        half, rows = self.rows // 2, self.rows
        self.wait("oA+")
        self.go("fA+", -1, 0, 0, half, self.nxt)
        self.wait("oB-")
        self.go("fB-", 1, 0, half, rows, self.prv)

    def step2(self):
        cross, ch = self.cross, self.cross // 2
        self.wait("oPA")
        self.go("pA+", 0, 1, 0, ch, self.nxt)
        self.wait("oPB")
        self.go("pB-", 0, 1, ch, cross, self.prv)
        self.go("pB+", 0, 1, ch, cross, self.nxt)
        self.go("pA-", 0, 1, 0, ch, self.prv)
        if cross < self.rows:
            self.wait("oP2")
        if self.core is not None:
            self.go("c01", 0, 1, 0, self.rows, self.core)

    def step3(self):
        rows, cross = self.rows, self.cross
        self.wait("oB+", "oA-")
        if cross < rows:
            self.go("y-", -1, 0, cross, rows, self.partner)
            self.go("y+", 1, 0, cross, rows, self.partner)
        if self.core is not None:
            self.go("c-0", -1, 0, 0, rows, self.core)
            self.go("c+0", 1, 0, 0, rows, self.core)

    def step4(self):
        rows, cross = self.rows, self.cross
        self.wait("fA+", "fB-")
        if cross < rows:
            self.go("y2", 2, 0, cross, rows, self.partner)
        if self.core is not None:
            self.go("c20", 2, 0, 0, rows, self.core)

    def step5(self):
        cross, ch = self.cross, self.cross // 2
        self.wait("pA+")
        self.go("qA+", -1, 1, 0, ch, self.nxt)
        self.wait("pB-")
        self.go("qB-", 1, 1, ch, cross, self.prv)

    def step6(self):
        self.wait("pB+", "pA-")
        if self.cross < self.rows:
            self.wait("y-", "y+")
        if self.core is not None:
            self.go("c-1", -1, 1, 0, self.rows, self.core)
            self.go("c+1", 1, 1, 0, self.rows, self.core)

    def step7(self):
        self.wait("qA+", "qB-")
        if self.cross < self.rows:
            self.wait("y2")
        if self.core is not None:
            self.go("c21", 2, 1, 0, self.rows, self.core)


def dp_of(z, yh, c):
    return lax.rem(z + 4, 4) * 4 + yh * 2 + c


def t_of(x, yl):
    return lax.rem(x + 4, 4) * 2 + yl


def grad_kernel(
    s_ref, c_ref, w_ref, m1_ref, m2_ref, upd_ref, new_ref,
    sb, cb, g, wv, m1v, m2v, send, recv, local,
):
    d, t, z, yh, c, x, yl = place()
    core = (d + 1 - 2 * c, t)
    yhp = (dp_of(z, 1 - yh, c), t)
    ylp = (d, t_of(x, 1 - yl))
    xn, xp = (d, t_of(x + 1, yl)), (d, t_of(x - 1, yl))
    zn, zp = (dp_of(z + 1, yh, c), t), (dp_of(z - 1, yh, c), t)
    others = [lax.rem(d + j, N_DP) for j in range(1, N_DP)]

    loads = [
        pltpu.make_async_copy(c_ref, cb.at[d], local.at[0]),
        pltpu.make_async_copy(
            s_ref.at[pl.ds(mo(t * SUB, SUB), SUB), pl.ds(mo(d * ROWS, ROWS), ROWS)],
            sb.at[t, pl.ds(mo(d * SUB, SUB), SUB), :],
            local.at[1],
        ),
        pltpu.make_async_copy(w_ref, wv, local.at[2]),
        pltpu.make_async_copy(m1_ref, m1v, local.at[3]),
        pltpu.make_async_copy(m2_ref, m2v, local.at[4]),
    ]
    for cp in loads:
        cp.start()
    greet([(e, t) for e in others] + [xn, xp, ylp])

    cps = Copies(send, recv)
    for j, e in enumerate(others):
        cps.start(
            ("a", j),
            s_ref.at[pl.ds(mo(t * SUB, SUB), SUB), pl.ds(mo(e * ROWS, ROWS), ROWS)],
            sb.at[t, pl.ds(mo(d * SUB, SUB), SUB), :],
            (e, t),
        )
    cot = Gather(
        "c", cps, cb, lambda rr, p: dp_of(z + rr, yh + p * (1 - 2 * yh), c),
        TOK, CROSS_C, zn, zp, yhp, core,
    )
    sta = Gather(
        "s", cps, sb, lambda rr, p: t_of(x + rr, yl + p * (1 - 2 * yl)),
        N_DP * SUB, CROSS_S, xn, xp, ylp,
    )
    cot.begin(c_ref)
    cps.arrived(*[("a", j) for j in range(N_DP - 1)])
    loads[1].wait()
    sta.begin()
    cot.step1()
    cot.step2()
    sta.step1()
    cot.step3()
    sta.step2()
    cot.step4()
    cot.step5()
    sta.step3()
    sta.step4()
    cot.step6()
    cot.step7()
    sta.step5()
    loads[0].wait()
    cps.arrived(*["c" + n for n in ("c00", "c01", "c-0", "c+0", "c20", "c-1", "c+1", "c21")])

    def term(tb):
        cc = cb[:, pl.ds(mo(tb * SUB, SUB), SUB), :].reshape(N_DP * SUB, SLICE)
        return lax.dot_general(
            sb[tb], cc, (((0,), (0,)), ((), ())), preferred_element_type=F32
        )

    g[...] = term(t)

    def ring(plane):
        def one(i, carry):
            g[...] += term(sta.index(i, plane))
            return carry

        return one

    lax.fori_loop(1, 4, ring(0), 0)
    g[...] += term(sta.index(0, 1))
    sta.step6()
    sta.step7()
    lax.fori_loop(1, 4, ring(1), 0)
    for cp in loads[2:]:
        cp.wait()

    def adam(i, carry):
        r = pl.ds(mo(i * 32, 32), 32)
        grad = g[r, :]
        moment = beta_one * m1v[r, :] + (1.0 - beta_one) * grad
        second = beta_two * m2v[r, :] + (1.0 - beta_two) * grad * grad
        upd = moment / bias_one / (jnp.sqrt(second / bias_two) + adam_eps)
        upd_ref[r, :] = upd
        new_ref[r, :] = (wv[r, :] - learn_rate * upd).astype(BF)
        return carry

    lax.fori_loop(0, ROWS // 32, adam, 0)
    cps.drain()


def block_kernel(
    new_ref, x_ref, gain_ref, wo_ref, cos_ref, sin_ref, out_ref,
    wb, nb, stage, acc, kv, att, woo, wop, part, r1, r2, fp,
    send, recv, send2, recv2, local,
):
    d, t, z, yh, c, x, yl = place()
    core = (d + 1 - 2 * c, t)
    yhp = (dp_of(z, 1 - yh, c), t)
    ylp = (d, t_of(x, 1 - yl))
    xn, xp = (d, t_of(x + 1, yl)), (d, t_of(x - 1, yl))
    zn, zp = (dp_of(z + 1, yh, c), t), (dp_of(z - 1, yh, c), t)
    mine = mo(yl * HALF, HALF)
    theirs = mo((1 - yl) * HALF, HALF)
    NR = 64

    def fetch(i):
        return pltpu.make_async_copy(
            x_ref.at[pl.ds(mo(i * NR, NR), NR), :], stage.at[lax.rem(i, 2)],
            local.at[lax.rem(i, 2)],
        )

    own = pltpu.make_async_copy(new_ref, wb.at[d], local.at[2])
    out_w = pltpu.make_async_copy(wo_ref.at[:, pl.ds(mine, HALF)], woo, local.at[3])
    fetch(0).start()
    own.start()
    greet([core, yhp, ylp, xn, xp, zn, zp])

    cps = Copies(send, recv)
    gat = Gather(
        "w", cps, wb, lambda rr, p: dp_of(z + rr, yh + p * (1 - 2 * yh), c),
        ROWS, CROSS_W, zn, zp, yhp, core,
    )
    gat.begin(new_ref)
    wrows = pl.ds(mo(c * (QW // 2), QW // 2), QW // 2)
    cps.start("wo", wo_ref.at[wrows, pl.ds(theirs, HALF)], wop.at[wrows, :], ylp)

    def norm(i, carry):
        @pl.when(i + 1 < LEN // NR)
        def _():
            fetch(i + 1).start()

        fetch(i).wait()
        slot = lax.rem(i, 2)

        def rows16(k, carry):
            r = pl.ds(mo(k * 16, 16), 16)
            ro = pl.ds(mo(i * NR + k * 16, 16), 16)
            tot = jnp.zeros((16, ROWS), F32)
            for j in range(N_DP):
                v = stage[slot, r, j * ROWS : (j + 1) * ROWS].astype(F32)
                tot = tot + v * v
            scale = lax.rsqrt(jnp.sum(tot, axis=1, keepdims=True) * (1.0 / D) + norm_eps)
            for j in range(N_DP):
                v = stage[slot, r, j * ROWS : (j + 1) * ROWS].astype(F32)
                gj = gain_ref[:, j * ROWS : (j + 1) * ROWS]
                nb[j, ro, :] = (v * scale * gj).astype(BF)
            return carry

        lax.fori_loop(0, NR // 16, rows16, 0)
        return carry

    lax.fori_loop(0, LEN // NR, norm, 0)
    out_w.start()

    def term(e):
        return jnp.dot(nb[e], wb[e], preferred_element_type=F32)

    def pair(rr, plane):
        base = dp_of(z + rr, yh + plane * (1 - 2 * yh), 0)

        def one(i, carry):
            acc[...] += term(base + i)
            return carry

        lax.fori_loop(0, 2, one, 0)

    own.wait()
    gat.step1()
    gat.step2()
    acc[...] = term(d)
    cps.arrived("wc00")
    acc[...] += term(d + 1 - 2 * c)
    gat.step3()
    gat.step4()
    cps.arrived("wc01")
    pair(0, 1)
    gat.step5()
    cps.arrived("wc-0", "wc+0", "wc20")

    def ring(plane):
        def one(i, carry):
            e = dp_of(z + 1 + i // 2, yh + plane * (1 - 2 * yh), lax.rem(i, 2))
            acc[...] += term(e)
            return carry

        lax.fori_loop(0, 6, one, 0)

    ring(0)
    cps.arrived("wo")
    cps.start("woc", wop.at[wrows, :], wop.at[wrows, :], core)
    gat.step6()
    gat.step7()
    cps.arrived("wc-1", "wc+1", "wc21")
    ring(1)

    def rope(u):
        return u * cos_ref[...] + pltpu.roll(u, HD // 2, 1) * sin_ref[...]

    kv[0] = rope(acc[:, QW : QW + HD]).astype(BF)
    kv[1] = acc[:, QW + HD :].astype(BF)
    HL = LEN // 2
    for h in range(QH):
        cols = slice(h * HD, (h + 1) * HD)
        q = (rope(acc[:, cols]) * (HD**-0.5)).astype(BF)
        for b in range(2):
            n = HL * (b + 1)
            s = lax.dot_general(
                q[b * HL : n], kv[0, :n], (((1,), (1,)), ((), ())),
                preferred_element_type=F32,
            )
            qi = lax.broadcasted_iota(jnp.int32, (HL, n), 0) + b * HL
            ki = lax.broadcasted_iota(jnp.int32, (HL, n), 1)
            s = jnp.where(qi >= ki, s, -jnp.inf)
            e = jnp.exp(s - jnp.max(s, axis=1, keepdims=True))
            a = (e / jnp.sum(e, axis=1, keepdims=True)).astype(BF)
            att[0, b * HL : n, cols] = jnp.dot(
                a, kv[1, :n], preferred_element_type=F32
            ).astype(BF)
        cps.start(("at", h), att.at[0, :, cols], att.at[1, :, cols], ylp)

    out_w.wait()
    cps.arrived("woc")
    cps.arrived(*[("at", h) for h in range(QH)])

    XB = LEN // 4
    HC = CW // 2

    def rows_of(xx):
        return pl.ds(mo(lax.rem(xx + 4, 4) * XB, XB), XB)

    def cols_of(k, w=CW, off=0):
        return pl.ds(mo(k * CW + off, HC), w)

    def remote(src, dst, i, peer):
        return pltpu.make_async_remote_copy(
            src_ref=src, dst_ref=dst, send_sem=send2.at[i], recv_sem=recv2.at[i],
            device_id=peer, device_id_type=MESH,
        )

    def far(k):
        hc = pl.ds(mo(k * HC, HC), HC)
        return (
            remote(part.at[rows_of(x + 2), cols_of(k, HC)], r1.at[0, :, hc], k, xn),
            remote(part.at[rows_of(x + 2), cols_of(k, HC, HC)], r1.at[1, :, hc], CHUNKS + k, xp),
        )

    def near(k):
        return (
            remote(part.at[rows_of(x + 1), cols_of(k)], r2.at[0, :, cols_of(k)], 2 * CHUNKS + k, xn),
            remote(part.at[rows_of(x - 1), cols_of(k)], r2.at[1, :, cols_of(k)], 3 * CHUNKS + k, xp),
        )

    def last(k):
        oc = pl.ds(mo(mine + k * CW, CW), CW)
        return remote(fp.at[:, cols_of(k)], out_ref.at[:, oc], 4 * CHUNKS + k, ylp)

    def produce(k, carry):
        def tile(j, carry):
            cc = pl.ds(mo(k * CW + j * 256, 256), 256)
            part[:, cc] = (
                jnp.dot(att[0], woo[:, cc], preferred_element_type=F32)
                + jnp.dot(att[1], wop[:, cc], preferred_element_type=F32)
            ).astype(BF)
            return carry

        lax.fori_loop(0, CW // 256, tile, 0)
        for cp in far(k):
            cp.start()
        return carry

    def forward(k, carry):
        hc = pl.ds(mo(k * HC, HC), HC)
        up, down = far(k)
        to_next, to_prev = near(k)
        for i, (cp, nx, rows, cc) in enumerate(
            (
                (up, to_next, rows_of(x + 1), cols_of(k, HC)),
                (down, to_prev, rows_of(x - 1), cols_of(k, HC, HC)),
            )
        ):
            cp.wait_recv()
            part[rows, cc] = (part[rows, cc].astype(F32) + r1[i, :, hc].astype(F32)).astype(BF)
            nx.start()
        return carry

    def finish(k, carry):
        to_next, to_prev = near(k)
        to_next.wait_recv()
        to_prev.wait_recv()
        SR = LEN // N_T

        def total(half):
            rows = pl.ds(mo(x * XB + half * SR, SR), SR)
            rr = pl.ds(mo(half * SR, SR), SR)
            cc = cols_of(k)
            return (
                part[rows, cc].astype(F32)
                + r2[0, rr, cc].astype(F32)
                + r2[1, rr, cc].astype(F32)
            ).astype(BF)

        fp[:, cols_of(k)] = total(1 - yl)
        last(k).start()
        out_ref[:, pl.ds(mo(mine + k * CW, CW), CW)] = total(yl)
        return carry

    def close(k, carry):
        for cp in far(k) + near(k):
            cp.wait_send()
        last(k).wait()
        return carry

    lax.fori_loop(0, CHUNKS, produce, 0)
    lax.fori_loop(0, CHUNKS, forward, 0)
    lax.fori_loop(0, CHUNKS, finish, 0)
    lax.fori_loop(0, CHUNKS, close, 0)
    cps.drain()


CROSS_C = TOK
CROSS_S = N_DP * SUB
CROSS_W = ROWS


def tables():
    half = HD // 2
    exponent = np.arange(half, dtype=np.float32) * np.float32(2.0 / HD)
    inverse = np.power(np.float64(rope_base), -exponent.astype(np.float64)).astype(np.float32)
    angles = np.arange(LEN, dtype=np.float32)[:, None] * inverse[None, :]
    cos = np.cos(angles.astype(np.float64)).astype(np.float32)
    sin = np.sin(angles.astype(np.float64)).astype(np.float32)
    return np.concatenate([cos, cos], 1), np.concatenate([-sin, sin], 1)


ANY = pl.BlockSpec(memory_space=pl.ANY)
VM = pl.BlockSpec(memory_space=pltpu.VMEM)


def body(
    train_states, qkv_cotangent, w_master, moment_one, moment_two, prompt_states, norm_gain, w_out
):
    dma = pltpu.SemaphoreType.DMA
    update_dir, fresh = pl.pallas_call(
        grad_kernel,
        name="grad_adam",
        out_shape=(
            jax.ShapeDtypeStruct((ROWS, SLICE), F32),
            jax.ShapeDtypeStruct((ROWS, SLICE), BF),
        ),
        in_specs=[ANY] * 5,
        out_specs=(VM, VM),
        scratch_shapes=[
            pltpu.VMEM((N_T, N_DP * SUB, ROWS), BF),
            pltpu.VMEM((N_DP, TOK, SLICE), BF),
            pltpu.VMEM((ROWS, SLICE), F32),
            pltpu.VMEM((ROWS, SLICE), F32),
            pltpu.VMEM((ROWS, SLICE), F32),
            pltpu.VMEM((ROWS, SLICE), F32),
            dma((64,)),
            dma((64,)),
            dma((5,)),
        ],
        compiler_params=pltpu.CompilerParams(
            collective_id=1, has_side_effects=True, vmem_limit_bytes=60 << 20
        ),
    )(train_states, qkv_cotangent, w_master, moment_one, moment_two)
    cos, sin = tables()
    out = pl.pallas_call(
        block_kernel,
        name="prefill",
        out_shape=jax.ShapeDtypeStruct((LEN // N_T, D), BF),
        in_specs=[ANY, ANY, VM, ANY, VM, VM],
        out_specs=VM,
        scratch_shapes=[
            pltpu.VMEM((N_DP, ROWS, SLICE), BF),
            pltpu.VMEM((N_DP, LEN, ROWS), BF),
            pltpu.VMEM((2, 64, D), BF),
            pltpu.VMEM((LEN, SLICE), F32),
            pltpu.VMEM((2, LEN, HD), BF),
            pltpu.VMEM((2, LEN, QW), BF),
            pltpu.VMEM((QW, HALF), BF),
            pltpu.VMEM((QW, HALF), BF),
            pltpu.VMEM((LEN, HALF), BF),
            pltpu.VMEM((2, LEN // 4, HALF // 2), BF),
            pltpu.VMEM((2, LEN // 4, HALF), BF),
            pltpu.VMEM((LEN // N_T, HALF), BF),
            dma((48,)),
            dma((48,)),
            dma((5 * CHUNKS,)),
            dma((5 * CHUNKS,)),
            dma((4,)),
        ],
        compiler_params=pltpu.CompilerParams(
            collective_id=2, has_side_effects=True, vmem_limit_bytes=63 << 20
        ),
    )(fresh, prompt_states, norm_gain.reshape(1, D), w_out, jnp.asarray(cos), jnp.asarray(sin))
    return (update_dir, out)


def solution(mesh):
    placed = (
        P("dp", None),
        P("dp", "tensor"),
        P("dp", "tensor"),
        P("dp", "tensor"),
        P("dp", "tensor"),
        P("dp", None),
        P(),
        P("tensor", None),
    )
    return jax.shard_map(
        body,
        mesh=mesh,
        in_specs=placed,
        out_specs=(P("dp", "tensor"), P(("dp", "tensor"), None)),
        check_vma=False,
    )
```

```python
import jax
import jax.numpy as jnp
import numpy as np
from jax import lax
from jax.experimental import pallas as pl
from jax.experimental.pallas import tpu as pltpu
from jax.sharding import PartitionSpec as P

HD = 128
QH = 4
LEN = 512
D = 8192
N_DP = 16
N_T = 8
SLICE = (QH + 2) * HD
QW = QH * HD
ROWS = D // N_DP
TOK = 256
SUB = TOK // N_T
HALF = D // 2
CHUNKS = 4
CW = HALF // CHUNKS
HR = ROWS // 2
NR = 32
N_COPIES = 200

beta_one = 0.9
beta_two = 0.95
bias_one = 1.0 - 0.9**8
bias_two = 1.0 - 0.95**8
learn_rate = 0.002
adam_eps = 1e-08
norm_eps = 1e-05
rope_base = 500000.0

MESH = pl.DeviceIdType.MESH
BF = jnp.bfloat16
F32 = jnp.float32


def place():
    d = lax.axis_index("dp")
    t = lax.axis_index("tensor")
    return d, t, d // 4, (d // 2) % 2, d % 2, t // 2, t % 2


def mo(v, m):
    return pl.multiple_of(v, m)


def greet(peers):
    barrier = pltpu.get_barrier_semaphore()
    for peer in peers:
        pl.semaphore_signal(barrier, inc=1, device_id=peer, device_id_type=MESH)
    pl.semaphore_wait(barrier, len(peers))


class Copies:
    def __init__(self, send, recv):
        self.send, self.recv, self.made, self.used = send, recv, {}, 0

    def start(self, name, src, dst, peer):
        cp = pltpu.make_async_remote_copy(
            src_ref=src,
            dst_ref=dst,
            send_sem=self.send.at[self.used],
            recv_sem=self.recv.at[self.used],
            device_id=peer,
            device_id_type=MESH,
        )
        self.used += 1
        self.made[name] = cp
        cp.start()

    def arrived(self, *names):
        for name in names:
            self.made[name].wait_recv()

    def drain(self):
        for cp in self.made.values():
            cp.wait_send()


class Gather:
    def __init__(self, tag, cps, buf, index, rows, cross, nxt, prv, partner, core=None):
        self.tag, self.cps, self.buf, self.index = tag, cps, buf, index
        self.rows, self.cross = rows, cross
        self.nxt, self.prv, self.partner, self.core = nxt, prv, partner, core

    def piece(self, rr, plane, lo, hi):
        return self.buf.at[self.index(rr, plane), pl.ds(lo, hi - lo), :]

    def go(self, name, rr, plane, lo, hi, peer, src=None):
        dst = self.piece(rr, plane, lo, hi)
        if src is None:
            src = dst
        self.cps.start(self.tag + (name,), src, dst, peer)

    def wait(self, *names):
        self.cps.arrived(*[self.tag + (name,) for name in names])

    def begin(self, own=None):
        rows, cross = self.rows, self.cross
        half, ch = rows // 2, self.cross // 2

        def src(lo, hi):
            if own is None:
                return None
            return own.at[pl.ds(lo, hi - lo), :]

        def send(name, lo, hi, peer):
            self.go(name, 0, 0, lo, hi, peer, src(lo, hi))

        send("oA+", 0, half, self.nxt)
        send("oB-", half, rows, self.prv)
        send("oPA", 0, ch, self.partner)
        send("oPB", ch, cross, self.partner)
        send("oB+", half, rows, self.nxt)
        send("oA-", 0, half, self.prv)
        if cross < rows:
            send("oP2", cross, rows, self.partner)
        if self.core is not None:
            send("c00", 0, rows, self.core)

    def step1(self):
        half, rows = self.rows // 2, self.rows
        self.wait("oA+")
        self.go("fA+", -1, 0, 0, half, self.nxt)
        self.wait("oB-")
        self.go("fB-", 1, 0, half, rows, self.prv)

    def step2(self):
        cross, ch = self.cross, self.cross // 2
        self.wait("oPA")
        self.go("pA+", 0, 1, 0, ch, self.nxt)
        self.wait("oPB")
        self.go("pB-", 0, 1, ch, cross, self.prv)
        self.go("pB+", 0, 1, ch, cross, self.nxt)
        self.go("pA-", 0, 1, 0, ch, self.prv)
        if cross < self.rows:
            self.wait("oP2")
        if self.core is not None:
            self.go("c01", 0, 1, 0, self.rows, self.core)

    def step3(self):
        rows, cross = self.rows, self.cross
        self.wait("oB+", "oA-")
        if cross < rows:
            self.go("y-", -1, 0, cross, rows, self.partner)
            self.go("y+", 1, 0, cross, rows, self.partner)
        if self.core is not None:
            self.go("c-0", -1, 0, 0, rows, self.core)
            self.go("c+0", 1, 0, 0, rows, self.core)

    def step4(self):
        rows, cross = self.rows, self.cross
        self.wait("fA+", "fB-")
        if cross < rows:
            self.go("y2", 2, 0, cross, rows, self.partner)
        if self.core is not None:
            self.go("c20", 2, 0, 0, rows, self.core)

    def step5(self):
        cross, ch = self.cross, self.cross // 2
        self.wait("pA+")
        self.go("qA+", -1, 1, 0, ch, self.nxt)
        self.wait("pB-")
        self.go("qB-", 1, 1, ch, cross, self.prv)

    def step6(self):
        self.wait("pB+", "pA-")
        if self.cross < self.rows:
            self.wait("y-", "y+")
        if self.core is not None:
            self.go("c-1", -1, 1, 0, self.rows, self.core)
            self.go("c+1", 1, 1, 0, self.rows, self.core)

    def step7(self):
        self.wait("qA+", "qB-")
        if self.cross < self.rows:
            self.wait("y2")
        if self.core is not None:
            self.go("c21", 2, 1, 0, self.rows, self.core)


def dp_of(z, yh, c):
    return lax.rem(z + 4, 4) * 4 + yh * 2 + c


def t_of(x, yl):
    return lax.rem(x + 4, 4) * 2 + yl


def kernel(
    s_ref, c_ref, w_ref, m1_ref, m2_ref, x_ref, gain_ref, wo_ref, cos_ref, sin_ref,
    upd_ref, out_ref,
    sb, cb, wv, m1v, m2v, wb, nb, stage, acc, kv, att, woo, wop, part, r1, r2, fp,
    send, recv, send2, recv2, local,
):
    d, t, z, yh, c, x, yl = place()
    core = (d + 1 - 2 * c, t)
    yhp = (dp_of(z, 1 - yh, c), t)
    ylp = (d, t_of(x, 1 - yl))
    far_y = lax.rem(2 * yh + yl + 3 + 2 * yl, 4)
    yfar = (dp_of(z, far_y // 2, c), t_of(x, lax.rem(far_y, 2)))
    xn, xp = (d, t_of(x + 1, yl)), (d, t_of(x - 1, yl))
    zn, zp = (dp_of(z + 1, yh, c), t), (dp_of(z - 1, yh, c), t)
    others = [lax.rem(d + j, N_DP) for j in range(1, N_DP)]
    mine = mo(yl * HALF, HALF)
    theirs = mo((1 - yl) * HALF, HALF)

    def spread(h, e):
        return s_ref.at[
            pl.ds(mo(t * SUB, SUB), SUB), pl.ds(mo(e * ROWS + h * HR, HR), HR)
        ]

    def landing(h):
        return sb.at[h, t, pl.ds(mo(d * SUB, SUB), SUB), :]

    def fetch(i):
        return pltpu.make_async_copy(
            x_ref.at[pl.ds(mo(i * NR, NR), NR), :], stage.at[lax.rem(i, 2)],
            local.at[lax.rem(i, 2)],
        )

    own_c = pltpu.make_async_copy(c_ref, cb.at[d], local.at[2])
    own_s = [pltpu.make_async_copy(spread(h, d), landing(h), local.at[3 + h]) for h in range(2)]
    state = [
        pltpu.make_async_copy(src, dst, local.at[5 + i])
        for i, (src, dst) in enumerate(((w_ref, wv), (m1_ref, m1v), (m2_ref, m2v)))
    ]
    out_w = pltpu.make_async_copy(wo_ref.at[:, pl.ds(mine, HALF)], woo, local.at[8])
    own_c.start()
    for cp in own_s:
        cp.start()
    fetch(0).start()
    greet([(e, t) for e in others] + [xn, xp, ylp, yfar])

    cps = Copies(send, recv)
    for h in range(2):
        for j, e in enumerate(others):
            cps.start(("a", h, j), spread(h, e), landing(h), (e, t))

    def dp_index(rr, p):
        return dp_of(z + rr, yh + p * (1 - 2 * yh), c)

    def t_index(rr, p):
        return t_of(x + rr, yl + p * (1 - 2 * yl))

    cot = Gather(("c",), cps, cb, dp_index, TOK, CROSS_C, zn, zp, yhp, core)
    sta = [
        Gather(("s", h), cps, sb.at[h], t_index, N_DP * SUB, CROSS_S, xn, xp, ylp)
        for h in range(2)
    ]
    gat = [
        Gather(("w", h), cps, wb.at[h], dp_index, HR, CROSS_W, zn, zp, yhp, core)
        for h in range(2)
    ]

    def norm(i, carry):
        @pl.when(i + 1 < LEN // NR)
        def _():
            fetch(i + 1).start()

        fetch(i).wait()
        slot = lax.rem(i, 2)

        def rows16(k, carry):
            r = pl.ds(mo(k * 16, 16), 16)
            ro = pl.ds(mo(i * NR + k * 16, 16), 16)
            tot = jnp.zeros((16, ROWS), F32)
            for j in range(N_DP):
                v = stage[slot, r, j * ROWS : (j + 1) * ROWS].astype(F32)
                tot = tot + v * v
            scale = lax.rsqrt(jnp.sum(tot, axis=1, keepdims=True) * (1.0 / D) + norm_eps)
            for j in range(N_DP):
                v = stage[slot, r, j * ROWS : (j + 1) * ROWS].astype(F32)
                gj = gain_ref[:, j * ROWS : (j + 1) * ROWS]
                nb[j, ro, :] = (v * scale * gj).astype(BF)
            return carry

        lax.fori_loop(0, NR // 16, rows16, 0)
        return carry

    def term(h, tb):
        cc = cb[:, pl.ds(mo(tb * SUB, SUB), SUB), :].reshape(N_DP * SUB, SLICE)
        return lax.dot_general(
            sb[h, tb], cc, (((0,), (0,)), ((), ())), preferred_element_type=F32
        )

    def gradient(h):
        rows = pl.ds(h * HR, HR)
        upd_ref[rows, :] = term(h, t)

        def one(i, carry):
            upd_ref[rows, :] += term(h, t_of(x + i // 2, lax.rem(yl + i, 2)))
            return carry

        lax.fori_loop(1, N_T, one, 0)

        def adam(i, carry):
            r = pl.ds(mo(h * HR + i * 32, 32), 32)
            grad = upd_ref[r, :]
            moment = beta_one * m1v[r, :] + (1.0 - beta_one) * grad
            second = beta_two * m2v[r, :] + (1.0 - beta_two) * grad * grad
            upd = moment / bias_one / (jnp.sqrt(second / bias_two) + adam_eps)
            upd_ref[r, :] = upd
            wb[h, d, pl.ds(mo(i * 32, 32), 32), :] = (wv[r, :] - learn_rate * upd).astype(BF)
            return carry

        lax.fori_loop(0, HR // 32, adam, 0)

    def project(h, rr, plane):
        e = dp_of(z + rr, yh + plane * (1 - 2 * yh), 0)
        hc = slice(h * HR, (h + 1) * HR)
        return jnp.dot(nb[e, :, hc], wb[h, e], preferred_element_type=F32) + jnp.dot(
            nb[e + 1, :, hc], wb[h, e + 1], preferred_element_type=F32
        )

    def project_ring(h, plane):
        def one(i, carry):
            acc[...] += project(h, i, plane)
            return carry

        lax.fori_loop(1, 4, one, 0)

    def here(h, *names):
        cps.arrived(*[("w", h) + (n,) for n in names])

    NN = LEN // NR
    for h in range(2):
        cps.arrived(*[("a", h, j) for j in range(N_DP - 1)])
        own_s[h].wait()
        if h == 0:
            sta[0].begin()
            cot.begin(c_ref)
            for cp in state:
                cp.start()
    lax.fori_loop(0, 1, norm, 0)
    sta[0].step1()
    cot.step1()
    cot.step2()
    sta[0].step2()
    wq = [pl.ds(mo((2 * c + i) * (QW // 4), QW // 4), QW // 4) for i in range(2)]
    for i, peer in enumerate((ylp, yfar)):
        cps.start(("o", i), wo_ref.at[wq[i], pl.ds(theirs, HALF)], wop.at[wq[i], :], peer)
    lax.fori_loop(1, 3, norm, 0)
    sta[0].step3()
    cot.step3()
    sta[0].step4()
    sta[0].step5()
    sta[1].begin()
    cot.step4()
    cot.step5()
    lax.fori_loop(3, 6, norm, 0)
    sta[0].step6()
    sta[0].step7()
    sta[1].step1()
    cot.step6()
    sta[1].step2()
    lax.fori_loop(6, NN, norm, 0)
    cot.step7()
    own_c.wait()
    for cp in state:
        cp.wait()
    cps.arrived(*[("c", n) for n in ("c00", "c01", "c-0", "c+0", "c20", "c-1", "c+1", "c21")])
    gradient(0)
    gat[0].begin()
    sta[1].step3()
    sta[1].step4()
    sta[1].step5()
    out_w.start()
    gat[0].step1()
    here(0, "c00")
    acc[...] = project(0, 0, 0)
    gat[0].step2()
    sta[1].step6()
    gat[0].step3()
    sta[1].step7()
    gradient(1)
    gat[0].step4()
    gat[0].step5()
    gat[1].begin()
    here(0, "c01")
    acc[...] += project(0, 0, 1)
    here(0, "c-0", "c+0", "c20")
    project_ring(0, 0)
    gat[0].step6()
    gat[1].step1()
    gat[1].step2()
    gat[0].step7()
    here(1, "c00", "c01")
    acc[...] += project(1, 0, 0)
    here(0, "c-1", "c+1", "c21")
    project_ring(0, 1)
    gat[1].step3()
    gat[1].step4()
    acc[...] += project(1, 0, 1)
    gat[1].step5()
    cps.arrived(("o", 0), ("o", 1))
    wc = pl.ds(mo(c * (QW // 2), QW // 2), QW // 2)
    cps.start("oc", wop.at[wc, :], wop.at[wc, :], core)
    here(1, "c-0", "c+0", "c20")
    project_ring(1, 0)
    gat[1].step6()
    gat[1].step7()
    here(1, "c-1", "c+1", "c21")
    project_ring(1, 1)

    def rope(u, rows):
        return u * cos_ref[rows, :] + pltpu.roll(u, HD // 2, 1) * sin_ref[rows, :]

    XB = LEN // 4
    HC = CW // 2
    whole = pl.ds(0, LEN)
    kv[0] = rope(acc[:, QW : QW + HD], whole).astype(BF)
    kv[1] = acc[:, QW + HD :].astype(BF)

    def rows_of(xx):
        return pl.ds(mo(lax.rem(xx + 4, 4) * XB, XB), XB)

    def attend(xx):
        rows = rows_of(xx)
        q = jnp.concatenate(
            [
                (rope(acc[rows, h * HD : (h + 1) * HD], rows) * (HD**-0.5)).astype(BF)
                for h in range(QH)
            ],
            axis=0,
        )
        s = lax.dot_general(
            q, kv[0], (((1,), (1,)), ((), ())), preferred_element_type=F32
        )
        qi = lax.broadcasted_iota(jnp.int32, (QH * XB, LEN), 0) % XB
        ki = lax.broadcasted_iota(jnp.int32, (QH * XB, LEN), 1)
        s = jnp.where(qi + lax.rem(xx + 4, 4) * XB >= ki, s, -jnp.inf)
        e = jnp.exp(s - jnp.max(s, axis=1, keepdims=True))
        a = (e * (1.0 / jnp.sum(e, axis=1, keepdims=True))).astype(BF)
        o = jnp.dot(a, kv[1], preferred_element_type=F32).astype(BF)
        for h in range(QH):
            att[0, rows, h * HD : (h + 1) * HD] = o[h * XB : (h + 1) * XB]

    def share(i, xx):
        rows = rows_of(xx)
        cps.start(("t", i), att.at[0, rows, :], att.at[1, rows, :], ylp)

    def cols_of(k, w=CW, off=0):
        return pl.ds(mo(k * CW + off, HC), w)

    def remote(src, dst, i, peer):
        return pltpu.make_async_remote_copy(
            src_ref=src, dst_ref=dst, send_sem=send2.at[i], recv_sem=recv2.at[i],
            device_id=peer, device_id_type=MESH,
        )

    def far(k):
        hc = pl.ds(mo(k * HC, HC), HC)
        return (
            remote(part.at[rows_of(x + 2), cols_of(k, HC)], r1.at[0, :, hc], k, xn),
            remote(part.at[rows_of(x + 2), cols_of(k, HC, HC)], r1.at[1, :, hc], CHUNKS + k, xp),
        )

    def near(k):
        return (
            remote(part.at[rows_of(x + 1), cols_of(k)], r2.at[0, :, cols_of(k)], 2 * CHUNKS + k, xn),
            remote(part.at[rows_of(x - 1), cols_of(k)], r2.at[1, :, cols_of(k)], 3 * CHUNKS + k, xp),
        )

    def last(k):
        oc = pl.ds(mo(mine + k * CW, CW), CW)
        return remote(fp.at[:, cols_of(k)], out_ref.at[:, oc], 4 * CHUNKS + k, ylp)

    def produce(xx, then=None):
        rows = rows_of(xx)

        def chunk(k, carry):
            def tile(j, carry):
                cc = pl.ds(mo(k * CW + j * 256, 256), 256)
                part[rows, cc] = (
                    jnp.dot(att[0, rows, :], woo[:, cc], preferred_element_type=F32)
                    + jnp.dot(att[1, rows, :], wop[:, cc], preferred_element_type=F32)
                ).astype(BF)
                return carry

            lax.fori_loop(0, CW // 256, tile, 0)
            if then is not None:
                then(k)
            return carry

        lax.fori_loop(0, CHUNKS, chunk, 0)

    def send_far(k):
        for cp in far(k):
            cp.start()

    def forward(k, carry):
        hc = pl.ds(mo(k * HC, HC), HC)
        up, down = far(k)
        to_next, to_prev = near(k)
        for i, (cp, nx, rows, cc) in enumerate(
            (
                (up, to_next, rows_of(x + 1), cols_of(k, HC)),
                (down, to_prev, rows_of(x - 1), cols_of(k, HC, HC)),
            )
        ):
            cp.wait_recv()
            part[rows, cc] = (part[rows, cc].astype(F32) + r1[i, :, hc].astype(F32)).astype(BF)
            nx.start()
        return carry

    def finish(k, carry):
        to_next, to_prev = near(k)
        to_next.wait_recv()
        to_prev.wait_recv()
        SR = LEN // N_T

        def total(half):
            rows = pl.ds(mo(x * XB + half * SR, SR), SR)
            rr = pl.ds(mo(half * SR, SR), SR)
            cc = cols_of(k)
            return (
                part[rows, cc].astype(F32)
                + r2[0, rr, cc].astype(F32)
                + r2[1, rr, cc].astype(F32)
            ).astype(BF)

        fp[:, cols_of(k)] = total(1 - yl)
        last(k).start()
        out_ref[:, pl.ds(mo(mine + k * CW, CW), CW)] = total(yl)
        return carry

    def close(k, carry):
        for cp in far(k) + near(k):
            cp.wait_send()
        last(k).wait()
        return carry

    attend(x + 2)
    share(0, x + 2)
    attend(x + 1)
    share(1, x + 1)
    out_w.wait()
    cps.arrived("oc", ("t", 0))
    produce(x + 2, send_far)
    attend(x - 1)
    share(2, x - 1)
    attend(x)
    share(3, x)
    cps.arrived(("t", 1))
    produce(x + 1)
    cps.arrived(("t", 2))
    produce(x - 1)
    lax.fori_loop(0, CHUNKS, forward, 0)
    cps.arrived(("t", 3))
    produce(x)
    lax.fori_loop(0, CHUNKS, finish, 0)
    lax.fori_loop(0, CHUNKS, close, 0)
    cps.drain()


CROSS_C = TOK
CROSS_S = N_DP * SUB
CROSS_W = HR


def tables():
    half = HD // 2
    exponent = np.arange(half, dtype=np.float32) * np.float32(2.0 / HD)
    inverse = np.power(np.float64(rope_base), -exponent.astype(np.float64)).astype(np.float32)
    angles = np.arange(LEN, dtype=np.float32)[:, None] * inverse[None, :]
    cos = np.cos(angles.astype(np.float64)).astype(np.float32)
    sin = np.sin(angles.astype(np.float64)).astype(np.float32)
    return np.concatenate([cos, cos], 1), np.concatenate([-sin, sin], 1)


ANY = pl.BlockSpec(memory_space=pl.ANY)
VM = pl.BlockSpec(memory_space=pltpu.VMEM)


def step(*args, name="adam_prefill"):
    dma = pltpu.SemaphoreType.DMA
    cos, sin = tables()
    return pl.pallas_call(
        kernel,
        name=name,
        out_shape=(
            jax.ShapeDtypeStruct((ROWS, SLICE), F32),
            jax.ShapeDtypeStruct((LEN // N_T, D), BF),
        ),
        in_specs=[ANY] * 6 + [VM, ANY, VM, VM],
        out_specs=(VM, VM),
        scratch_shapes=[
            pltpu.VMEM((2, N_T, N_DP * SUB, HR), BF),
            pltpu.VMEM((N_DP, TOK, SLICE), BF),
            pltpu.VMEM((ROWS, SLICE), F32),
            pltpu.VMEM((ROWS, SLICE), F32),
            pltpu.VMEM((ROWS, SLICE), F32),
            pltpu.VMEM((2, N_DP, HR, SLICE), BF),
            pltpu.VMEM((N_DP, LEN, ROWS), BF),
            pltpu.VMEM((2, NR, D), BF),
            pltpu.VMEM((LEN, SLICE), F32),
            pltpu.VMEM((2, LEN, HD), BF),
            pltpu.VMEM((2, LEN, QW), BF),
            pltpu.VMEM((QW, HALF), BF),
            pltpu.VMEM((QW, HALF), BF),
            pltpu.VMEM((LEN, HALF), BF),
            pltpu.VMEM((2, LEN // 4, HALF // 2), BF),
            pltpu.VMEM((2, LEN // 4, HALF), BF),
            pltpu.VMEM((LEN // N_T, HALF), BF),
            dma((N_COPIES,)),
            dma((N_COPIES,)),
            dma((5 * CHUNKS,)),
            dma((5 * CHUNKS,)),
            dma((9,)),
        ],
        compiler_params=pltpu.CompilerParams(
            collective_id=1, has_side_effects=True, vmem_limit_bytes=67043328
        ),
    )(*args[:6], args[6].reshape(1, D), args[7], jnp.asarray(cos), jnp.asarray(sin))


def body(
    train_states, qkv_cotangent, w_master, moment_one, moment_two, prompt_states, norm_gain, w_out
):
    return step(
        train_states, qkv_cotangent, w_master, moment_one, moment_two,
        prompt_states, norm_gain, w_out,
    )


def solution(mesh):
    placed = (
        P("dp", None),
        P("dp", "tensor"),
        P("dp", "tensor"),
        P("dp", "tensor"),
        P("dp", "tensor"),
        P("dp", None),
        P(),
        P("tensor", None),
    )
    return jax.shard_map(
        body,
        mesh=mesh,
        in_specs=placed,
        out_specs=(P("dp", "tensor"), P(("dp", "tensor"), None)),
        check_vma=False,
    )
```

```python
import jax
import jax.numpy as jnp
import numpy as np
from jax import lax
from jax.experimental import pallas as pl
from jax.experimental.pallas import tpu as pltpu
from jax.sharding import PartitionSpec as P

HD = 128
QH = 4
LEN = 512
D = 8192
N_DP = 16
N_T = 8
SLICE = (QH + 2) * HD
QW = QH * HD
ROWS = D // N_DP
TOK = 256
SUB = TOK // N_T
HALF = D // 2
CHUNKS = 4
CW = HALF // CHUNKS
HR = ROWS // 2
NR = 32
N_COPIES = 200

beta_one = 0.9
beta_two = 0.95
bias_one = 1.0 - 0.9**8
bias_two = 1.0 - 0.95**8
learn_rate = 0.002
adam_eps = 1e-08
norm_eps = 1e-05
rope_base = 500000.0

MESH = pl.DeviceIdType.MESH
BF = jnp.bfloat16
F32 = jnp.float32


def place():
    d = lax.axis_index("dp")
    t = lax.axis_index("tensor")
    return d, t, d // 4, (d // 2) % 2, d % 2, t // 2, t % 2


def mo(v, m):
    return pl.multiple_of(v, m)


def greet(peers):
    barrier = pltpu.get_barrier_semaphore()
    for peer in peers:
        pl.semaphore_signal(barrier, inc=1, device_id=peer, device_id_type=MESH)
    pl.semaphore_wait(barrier, len(peers))


class Copies:
    def __init__(self, send, recv):
        self.send, self.recv, self.made, self.used = send, recv, {}, 0

    def start(self, name, src, dst, peer):
        cp = pltpu.make_async_remote_copy(
            src_ref=src,
            dst_ref=dst,
            send_sem=self.send.at[self.used],
            recv_sem=self.recv.at[self.used],
            device_id=peer,
            device_id_type=MESH,
        )
        self.used += 1
        self.made[name] = cp
        cp.start()

    def arrived(self, *names):
        for name in names:
            self.made[name].wait_recv()

    def drain(self):
        for cp in self.made.values():
            cp.wait_send()


class Gather:
    def __init__(
        self, tag, cps, buf, index, rows, cross, nxt, prv, partner, core=None, cols=None
    ):
        self.tag, self.cps, self.buf, self.index = tag, cps, buf, index
        self.rows, self.cross = rows, cross
        self.nxt, self.prv, self.partner, self.core = nxt, prv, partner, core
        self.cols = slice(None) if cols is None else pl.ds(*cols)

    def piece(self, rr, plane, lo, hi):
        return self.buf.at[self.index(rr, plane), pl.ds(lo, hi - lo), self.cols]

    def go(self, name, rr, plane, lo, hi, peer, src=None):
        dst = self.piece(rr, plane, lo, hi)
        if src is None:
            src = dst
        self.cps.start(self.tag + (name,), src, dst, peer)

    def wait(self, *names):
        self.cps.arrived(*[self.tag + (name,) for name in names])

    def begin(self, own=None):
        rows, cross = self.rows, self.cross
        half, ch = rows // 2, self.cross // 2

        def src(lo, hi):
            if own is None:
                return None
            return own.at[pl.ds(lo, hi - lo), :]

        def send(name, lo, hi, peer):
            self.go(name, 0, 0, lo, hi, peer, src(lo, hi))

        send("oA+", 0, half, self.nxt)
        send("oB-", half, rows, self.prv)
        send("oPA", 0, ch, self.partner)
        send("oPB", ch, cross, self.partner)
        send("oB+", half, rows, self.nxt)
        send("oA-", 0, half, self.prv)
        if cross < rows:
            send("oP2", cross, rows, self.partner)
        if self.core is not None:
            send("c00", 0, rows, self.core)

    def step1(self):
        half, rows = self.rows // 2, self.rows
        self.wait("oA+")
        self.go("fA+", -1, 0, 0, half, self.nxt)
        self.wait("oB-")
        self.go("fB-", 1, 0, half, rows, self.prv)

    def step2(self):
        cross, ch = self.cross, self.cross // 2
        self.wait("oPA")
        self.go("pA+", 0, 1, 0, ch, self.nxt)
        self.wait("oPB")
        self.go("pB-", 0, 1, ch, cross, self.prv)
        self.go("pB+", 0, 1, ch, cross, self.nxt)
        self.go("pA-", 0, 1, 0, ch, self.prv)
        if cross < self.rows:
            self.wait("oP2")
        if self.core is not None:
            self.go("c01", 0, 1, 0, self.rows, self.core)

    def step3(self):
        rows, cross = self.rows, self.cross
        self.wait("oB+", "oA-")
        if cross < rows:
            self.go("y-", -1, 0, cross, rows, self.partner)
            self.go("y+", 1, 0, cross, rows, self.partner)
        if self.core is not None:
            self.go("c-0", -1, 0, 0, rows, self.core)
            self.go("c+0", 1, 0, 0, rows, self.core)

    def step4(self):
        rows, cross = self.rows, self.cross
        self.wait("fA+", "fB-")
        if cross < rows:
            self.go("y2", 2, 0, cross, rows, self.partner)
        if self.core is not None:
            self.go("c20", 2, 0, 0, rows, self.core)

    def step5(self):
        cross, ch = self.cross, self.cross // 2
        self.wait("pA+")
        self.go("qA+", -1, 1, 0, ch, self.nxt)
        self.wait("pB-")
        self.go("qB-", 1, 1, ch, cross, self.prv)

    def step6(self):
        self.wait("pB+", "pA-")
        if self.cross < self.rows:
            self.wait("y-", "y+")
        if self.core is not None:
            self.go("c-1", -1, 1, 0, self.rows, self.core)
            self.go("c+1", 1, 1, 0, self.rows, self.core)

    def step7(self):
        self.wait("qA+", "qB-")
        if self.cross < self.rows:
            self.wait("y2")
        if self.core is not None:
            self.go("c21", 2, 1, 0, self.rows, self.core)


def dp_of(z, yh, c):
    return lax.rem(z + 4, 4) * 4 + yh * 2 + c


def t_of(x, yl):
    return lax.rem(x + 4, 4) * 2 + yl


def kernel(
    s_ref, c_ref, w_ref, m1_ref, m2_ref, x_ref, gain_ref, wo_ref, cos_ref, sin_ref,
    upd_ref, out_ref,
    sv, sb, cb, wv, m1v, m2v, wb, nb, stage, acc, kv, att, woo, wop, part, r1, r2, fp,
    send, recv, send2, recv2, local,
):
    d, t, z, yh, c, x, yl = place()
    core = (d + 1 - 2 * c, t)
    yhp = (dp_of(z, 1 - yh, c), t)
    ylp = (d, t_of(x, 1 - yl))
    far_y = lax.rem(2 * yh + yl + 3 + 2 * yl, 4)
    yfar = (dp_of(z, far_y // 2, c), t_of(x, lax.rem(far_y, 2)))
    xn, xp = (d, t_of(x + 1, yl)), (d, t_of(x - 1, yl))
    zn, zp = (dp_of(z + 1, yh, c), t), (dp_of(z - 1, yh, c), t)
    others = [lax.rem(d + j, N_DP) for j in range(1, N_DP)]
    mine = mo(yl * HALF, HALF)
    theirs = mo((1 - yl) * HALF, HALF)

    def spread(e):
        return sv.at[:, pl.ds(mo(e * ROWS, ROWS), ROWS)]

    landing = sb.at[t, pl.ds(mo(d * SUB, SUB), SUB), :]

    def fetch(i):
        return pltpu.make_async_copy(
            x_ref.at[pl.ds(mo(i * NR, NR), NR), :], stage.at[lax.rem(i, 2)],
            local.at[lax.rem(i, 2)],
        )

    own_c = pltpu.make_async_copy(c_ref, cb.at[d], local.at[2])
    load_s = pltpu.make_async_copy(s_ref.at[pl.ds(mo(t * SUB, SUB), SUB), :], sv, local.at[3])
    own_s = pltpu.make_async_copy(spread(d), landing, local.at[4])
    state = [
        pltpu.make_async_copy(src, dst, local.at[5 + i])
        for i, (src, dst) in enumerate(((w_ref, wv), (m1_ref, m1v), (m2_ref, m2v)))
    ]
    out_w = pltpu.make_async_copy(wo_ref.at[:, pl.ds(mine, HALF)], woo, local.at[8])
    load_s.start()
    own_c.start()
    fetch(0).start()
    greet([(e, t) for e in others] + [xn, xp, ylp, yfar])
    load_s.wait()

    cps = Copies(send, recv)

    def dp_index(rr, p):
        return dp_of(z + rr, yh + p * (1 - 2 * yh), c)

    def t_index(rr, p):
        return t_of(x + rr, yl + p * (1 - 2 * yl))

    cot = Gather(("c",), cps, cb, dp_index, TOK, CROSS_C, zn, zp, yhp, core)
    sta = [
        Gather(("s", h), cps, sb, t_index, N_DP * SUB, CROSS_S, xn, xp, ylp, None, (h * HR, HR))
        for h in range(2)
    ]
    gat = [
        Gather(("w", h), cps, wb.at[h], dp_index, HR, CROSS_W, zn, zp, yhp, core)
        for h in range(2)
    ]

    def norm(i, carry):
        @pl.when(i + 1 < LEN // NR)
        def _():
            fetch(i + 1).start()

        fetch(i).wait()
        slot = lax.rem(i, 2)

        def rows16(k, carry):
            r = pl.ds(mo(k * 16, 16), 16)
            ro = pl.ds(mo(i * NR + k * 16, 16), 16)
            tot = jnp.zeros((16, ROWS), F32)
            for j in range(N_DP):
                v = stage[slot, r, j * ROWS : (j + 1) * ROWS].astype(F32)
                tot = tot + v * v
            scale = lax.rsqrt(jnp.sum(tot, axis=1, keepdims=True) * (1.0 / D) + norm_eps)
            for j in range(N_DP):
                v = stage[slot, r, j * ROWS : (j + 1) * ROWS].astype(F32)
                gj = gain_ref[:, j * ROWS : (j + 1) * ROWS]
                nb[j, ro, :] = (v * scale * gj).astype(BF)
            return carry

        lax.fori_loop(0, NR // 16, rows16, 0)
        return carry

    def term(h, tb):
        cc = cb[:, pl.ds(mo(tb * SUB, SUB), SUB), :].reshape(N_DP * SUB, SLICE)
        return lax.dot_general(
            sb[tb, :, h * HR : (h + 1) * HR], cc, (((0,), (0,)), ((), ())), preferred_element_type=F32
        )

    def gradient(h):
        rows = pl.ds(h * HR, HR)
        upd_ref[rows, :] = term(h, t)

        def one(i, carry):
            upd_ref[rows, :] += term(h, t_of(x + i // 2, lax.rem(yl + i, 2)))
            return carry

        lax.fori_loop(1, N_T, one, 0)

        def adam(i, carry):
            r = pl.ds(mo(h * HR + i * 32, 32), 32)
            grad = upd_ref[r, :]
            moment = beta_one * m1v[r, :] + (1.0 - beta_one) * grad
            second = beta_two * m2v[r, :] + (1.0 - beta_two) * grad * grad
            upd = moment / bias_one / (jnp.sqrt(second / bias_two) + adam_eps)
            upd_ref[r, :] = upd
            wb[h, d, pl.ds(mo(i * 32, 32), 32), :] = (wv[r, :] - learn_rate * upd).astype(BF)
            return carry

        lax.fori_loop(0, HR // 32, adam, 0)

    def project(h, rr, plane):
        e = dp_of(z + rr, yh + plane * (1 - 2 * yh), 0)
        hc = slice(h * HR, (h + 1) * HR)
        return jnp.dot(nb[e, :, hc], wb[h, e], preferred_element_type=F32) + jnp.dot(
            nb[e + 1, :, hc], wb[h, e + 1], preferred_element_type=F32
        )

    def project_ring(h, plane):
        def one(i, carry):
            acc[...] += project(h, i, plane)
            return carry

        lax.fori_loop(1, 4, one, 0)

    def here(h, *names):
        cps.arrived(*[("w", h) + (n,) for n in names])

    NN = LEN // NR
    for j, e in enumerate(others):
        cps.start(("a", j), spread(e), landing, (e, t))
    own_s.start()
    cot.begin(c_ref)
    for cp in state:
        cp.start()
    lax.fori_loop(0, 7, norm, 0)
    cps.arrived(*[("a", j) for j in range(N_DP - 1)])
    own_s.wait()
    sta[0].begin()
    cot.step1()
    sta[0].step1()
    cot.step2()
    sta[0].step2()
    sta[0].step3()
    cot.step3()
    sta[0].step4()
    cot.step4()
    sta[0].step5()
    sta[1].begin()
    cot.step5()
    lax.fori_loop(7, NN, norm, 0)
    sta[0].step6()
    cot.step6()
    cot.step7()
    sta[0].step7()
    own_c.wait()
    for cp in state:
        cp.wait()
    cps.arrived(*[("c", n) for n in ("c00", "c01", "c-0", "c+0", "c20", "c-1", "c+1", "c21")])
    gradient(0)
    gat[0].begin()
    wq = [pl.ds(mo((2 * c + i) * (QW // 4), QW // 4), QW // 4) for i in range(2)]
    for i, peer in enumerate((ylp, yfar)):
        cps.start(("o", i), wo_ref.at[wq[i], pl.ds(theirs, HALF)], wop.at[wq[i], :], peer)
    sta[1].step1()
    sta[1].step2()
    out_w.start()
    gat[0].step1()
    gat[0].step2()
    sta[1].step3()
    sta[1].step4()
    gat[0].step3()
    sta[1].step5()
    here(0, "c00")
    acc[...] = project(0, 0, 0)
    gat[0].step4()
    sta[1].step6()
    gat[0].step5()
    sta[1].step7()
    gradient(1)
    gat[1].begin()
    here(0, "c01")
    acc[...] += project(0, 0, 1)
    here(0, "c-0", "c+0", "c20")
    project_ring(0, 0)
    gat[0].step6()
    gat[0].step7()
    gat[1].step1()
    gat[1].step2()
    here(0, "c-1", "c+1", "c21")
    project_ring(0, 1)
    gat[1].step3()
    here(1, "c00", "c01")
    acc[...] += project(1, 0, 0)
    gat[1].step4()
    acc[...] += project(1, 0, 1)
    gat[1].step5()
    cps.arrived(("o", 0), ("o", 1))
    wc = pl.ds(mo(c * (QW // 2), QW // 2), QW // 2)
    cps.start("oc", wop.at[wc, :], wop.at[wc, :], core)
    gat[1].step6()
    here(1, "c-0", "c+0", "c20")
    project_ring(1, 0)
    gat[1].step7()
    here(1, "c-1", "c+1", "c21")
    project_ring(1, 1)

    def rope(u, rows):
        return u * cos_ref[rows, :] + pltpu.roll(u, HD // 2, 1) * sin_ref[rows, :]

    XB = LEN // 4
    HC = CW // 2
    whole = pl.ds(0, LEN)
    kv[0] = rope(acc[:, QW : QW + HD], whole).astype(BF)
    kv[1] = acc[:, QW + HD :].astype(BF)

    def rows_of(xx):
        return pl.ds(mo(lax.rem(xx + 4, 4) * XB, XB), XB)

    def attend(xx):
        rows = rows_of(xx)
        q = jnp.concatenate(
            [
                (rope(acc[rows, h * HD : (h + 1) * HD], rows) * (HD**-0.5)).astype(BF)
                for h in range(QH)
            ],
            axis=0,
        )
        s = lax.dot_general(
            q, kv[0], (((1,), (1,)), ((), ())), preferred_element_type=F32
        )
        qi = lax.broadcasted_iota(jnp.int32, (QH * XB, LEN), 0) % XB
        ki = lax.broadcasted_iota(jnp.int32, (QH * XB, LEN), 1)
        s = jnp.where(qi + lax.rem(xx + 4, 4) * XB >= ki, s, -jnp.inf)
        e = jnp.exp(s - jnp.max(s, axis=1, keepdims=True))
        a = (e * (1.0 / jnp.sum(e, axis=1, keepdims=True))).astype(BF)
        o = jnp.dot(a, kv[1], preferred_element_type=F32).astype(BF)
        for h in range(QH):
            att[0, rows, h * HD : (h + 1) * HD] = o[h * XB : (h + 1) * XB]

    def share(i, xx):
        rows = rows_of(xx)
        cps.start(("t", i), att.at[0, rows, :], att.at[1, rows, :], ylp)

    def cols_of(k, w=CW, off=0):
        return pl.ds(mo(k * CW + off, HC), w)

    def remote(src, dst, i, peer):
        return pltpu.make_async_remote_copy(
            src_ref=src, dst_ref=dst, send_sem=send2.at[i], recv_sem=recv2.at[i],
            device_id=peer, device_id_type=MESH,
        )

    def far(k):
        hc = pl.ds(mo(k * HC, HC), HC)
        return (
            remote(part.at[rows_of(x + 2), cols_of(k, HC)], r1.at[0, :, hc], k, xn),
            remote(part.at[rows_of(x + 2), cols_of(k, HC, HC)], r1.at[1, :, hc], CHUNKS + k, xp),
        )

    def near(k):
        return (
            remote(part.at[rows_of(x + 1), cols_of(k)], r2.at[0, :, cols_of(k)], 2 * CHUNKS + k, xn),
            remote(part.at[rows_of(x - 1), cols_of(k)], r2.at[1, :, cols_of(k)], 3 * CHUNKS + k, xp),
        )

    def last(k):
        oc = pl.ds(mo(mine + k * CW, CW), CW)
        return remote(fp.at[:, cols_of(k)], out_ref.at[:, oc], 4 * CHUNKS + k, ylp)

    def produce(xx, then=None):
        rows = rows_of(xx)

        def chunk(k, carry):
            def tile(j, carry):
                cc = pl.ds(mo(k * CW + j * 256, 256), 256)
                part[rows, cc] = (
                    jnp.dot(att[0, rows, :], woo[:, cc], preferred_element_type=F32)
                    + jnp.dot(att[1, rows, :], wop[:, cc], preferred_element_type=F32)
                ).astype(BF)
                return carry

            lax.fori_loop(0, CW // 256, tile, 0)
            if then is not None:
                then(k)
            return carry

        lax.fori_loop(0, CHUNKS, chunk, 0)

    def send_far(k):
        for cp in far(k):
            cp.start()

    def forward(k, carry):
        hc = pl.ds(mo(k * HC, HC), HC)
        up, down = far(k)
        to_next, to_prev = near(k)
        for i, (cp, nx, rows, cc) in enumerate(
            (
                (up, to_next, rows_of(x + 1), cols_of(k, HC)),
                (down, to_prev, rows_of(x - 1), cols_of(k, HC, HC)),
            )
        ):
            cp.wait_recv()
            part[rows, cc] = (part[rows, cc].astype(F32) + r1[i, :, hc].astype(F32)).astype(BF)
            nx.start()
        return carry

    def finish(k, carry):
        to_next, to_prev = near(k)
        to_next.wait_recv()
        to_prev.wait_recv()
        SR = LEN // N_T

        def total(half):
            rows = pl.ds(mo(x * XB + half * SR, SR), SR)
            rr = pl.ds(mo(half * SR, SR), SR)
            cc = cols_of(k)
            return (
                part[rows, cc].astype(F32)
                + r2[0, rr, cc].astype(F32)
                + r2[1, rr, cc].astype(F32)
            ).astype(BF)

        fp[:, cols_of(k)] = total(1 - yl)
        last(k).start()
        out_ref[:, pl.ds(mo(mine + k * CW, CW), CW)] = total(yl)
        return carry

    def close(k, carry):
        for cp in far(k) + near(k):
            cp.wait_send()
        last(k).wait()
        return carry

    attend(x + 2)
    share(0, x + 2)
    attend(x + 1)
    share(1, x + 1)
    out_w.wait()
    cps.arrived("oc", ("t", 0))
    produce(x + 2, send_far)
    attend(x - 1)
    share(2, x - 1)
    attend(x)
    share(3, x)
    cps.arrived(("t", 1))
    produce(x + 1)
    cps.arrived(("t", 2))
    produce(x - 1)
    lax.fori_loop(0, CHUNKS, forward, 0)
    cps.arrived(("t", 3))
    produce(x)
    lax.fori_loop(0, CHUNKS, finish, 0)
    lax.fori_loop(0, CHUNKS, close, 0)
    cps.drain()


CROSS_C = 160
CROSS_S = N_DP * SUB
CROSS_W = 224


def tables():
    half = HD // 2
    exponent = np.arange(half, dtype=np.float32) * np.float32(2.0 / HD)
    inverse = np.power(np.float64(rope_base), -exponent.astype(np.float64)).astype(np.float32)
    angles = np.arange(LEN, dtype=np.float32)[:, None] * inverse[None, :]
    cos = np.cos(angles.astype(np.float64)).astype(np.float32)
    sin = np.sin(angles.astype(np.float64)).astype(np.float32)
    return np.concatenate([cos, cos], 1), np.concatenate([-sin, sin], 1)


ANY = pl.BlockSpec(memory_space=pl.ANY)
VM = pl.BlockSpec(memory_space=pltpu.VMEM)


def step(*args, name="adam_prefill"):
    dma = pltpu.SemaphoreType.DMA
    cos, sin = tables()
    return pl.pallas_call(
        kernel,
        name=name,
        out_shape=(
            jax.ShapeDtypeStruct((ROWS, SLICE), F32),
            jax.ShapeDtypeStruct((LEN // N_T, D), BF),
        ),
        in_specs=[ANY] * 6 + [VM, ANY, VM, VM],
        out_specs=(VM, VM),
        scratch_shapes=[
            pltpu.VMEM((SUB, D), BF),
            pltpu.VMEM((N_T, N_DP * SUB, ROWS), BF),
            pltpu.VMEM((N_DP, TOK, SLICE), BF),
            pltpu.VMEM((ROWS, SLICE), F32),
            pltpu.VMEM((ROWS, SLICE), F32),
            pltpu.VMEM((ROWS, SLICE), F32),
            pltpu.VMEM((2, N_DP, HR, SLICE), BF),
            pltpu.VMEM((N_DP, LEN, ROWS), BF),
            pltpu.VMEM((2, NR, D), BF),
            pltpu.VMEM((LEN, SLICE), F32),
            pltpu.VMEM((2, LEN, HD), BF),
            pltpu.VMEM((2, LEN, QW), BF),
            pltpu.VMEM((QW, HALF), BF),
            pltpu.VMEM((QW, HALF), BF),
            pltpu.VMEM((LEN, HALF), BF),
            pltpu.VMEM((2, LEN // 4, HALF // 2), BF),
            pltpu.VMEM((2, LEN // 4, HALF), BF),
            pltpu.VMEM((LEN // N_T, HALF), BF),
            dma((N_COPIES,)),
            dma((N_COPIES,)),
            dma((5 * CHUNKS,)),
            dma((5 * CHUNKS,)),
            dma((9,)),
        ],
        compiler_params=pltpu.CompilerParams(
            collective_id=1, has_side_effects=True, vmem_limit_bytes=67043328
        ),
    )(*args[:6], args[6].reshape(1, D), args[7], jnp.asarray(cos), jnp.asarray(sin))


def body(
    train_states, qkv_cotangent, w_master, moment_one, moment_two, prompt_states, norm_gain, w_out
):
    return step(
        train_states, qkv_cotangent, w_master, moment_one, moment_two,
        prompt_states, norm_gain, w_out,
    )


def solution(mesh):
    placed = (
        P("dp", None),
        P("dp", "tensor"),
        P("dp", "tensor"),
        P("dp", "tensor"),
        P("dp", "tensor"),
        P("dp", None),
        P(),
        P("tensor", None),
    )
    return jax.shard_map(
        body,
        mesh=mesh,
        in_specs=placed,
        out_specs=(P("dp", "tensor"), P(("dp", "tensor"), None)),
        check_vma=False,
    )
```

```python
import jax
import jax.numpy as jnp
import numpy as np
from jax import lax
from jax.experimental import pallas as pl
from jax.experimental.pallas import tpu as pltpu
from jax.sharding import PartitionSpec as P

HD = 128
QH = 4
LEN = 512
D = 8192
N_DP = 16
N_T = 8
SLICE = (QH + 2) * HD
QW = QH * HD
ROWS = D // N_DP
TOK = 256
SUB = TOK // N_T
HALF = D // 2
CHUNKS = 4
CW = HALF // CHUNKS
HR = ROWS // 2
NR = 32
N_COPIES = 200

beta_one = 0.9
beta_two = 0.95
bias_one = 1.0 - 0.9**8
bias_two = 1.0 - 0.95**8
learn_rate = 0.002
adam_eps = 1e-08
norm_eps = 1e-05
rope_base = 500000.0

MESH = pl.DeviceIdType.MESH
BF = jnp.bfloat16
F32 = jnp.float32


def place():
    d = lax.axis_index("dp")
    t = lax.axis_index("tensor")
    return d, t, d // 4, (d // 2) % 2, d % 2, t // 2, t % 2


def mo(v, m):
    return pl.multiple_of(v, m)


def greet(peers):
    barrier = pltpu.get_barrier_semaphore()
    for peer in peers:
        pl.semaphore_signal(barrier, inc=1, device_id=peer, device_id_type=MESH)
    pl.semaphore_wait(barrier, len(peers))


class Copies:
    def __init__(self, send, recv):
        self.send, self.recv, self.made, self.used = send, recv, {}, 0

    def start(self, name, src, dst, peer):
        cp = pltpu.make_async_remote_copy(
            src_ref=src,
            dst_ref=dst,
            send_sem=self.send.at[self.used],
            recv_sem=self.recv.at[self.used],
            device_id=peer,
            device_id_type=MESH,
        )
        self.used += 1
        self.made[name] = cp
        cp.start()

    def arrived(self, *names):
        for name in names:
            self.made[name].wait_recv()

    def drain(self):
        for cp in self.made.values():
            cp.wait_send()


class Gather:
    def __init__(
        self, tag, cps, buf, index, rows, cross, nxt, prv, partner, core=None
    ):
        self.tag, self.cps, self.buf, self.index = tag, cps, buf, index
        self.rows, self.cross = rows, cross
        self.nxt, self.prv, self.partner, self.core = nxt, prv, partner, core

    def piece(self, rr, plane, lo, hi):
        return self.buf.at[self.index(rr, plane), pl.ds(lo, hi - lo), :]

    def go(self, name, rr, plane, lo, hi, peer, src=None):
        dst = self.piece(rr, plane, lo, hi)
        if src is None:
            src = dst
        self.cps.start(self.tag + (name,), src, dst, peer)

    def wait(self, *names):
        self.cps.arrived(*[self.tag + (name,) for name in names])

    def begin(self, own=None):
        rows, cross = self.rows, self.cross
        half, ch = rows // 2, self.cross // 2

        def src(lo, hi):
            if own is None:
                return None
            return own.at[pl.ds(lo, hi - lo), :]

        def send(name, lo, hi, peer):
            self.go(name, 0, 0, lo, hi, peer, src(lo, hi))

        send("oA+", 0, half, self.nxt)
        send("oB-", half, rows, self.prv)
        send("oPA", 0, ch, self.partner)
        send("oPB", ch, cross, self.partner)
        send("oB+", half, rows, self.nxt)
        send("oA-", 0, half, self.prv)
        if cross < rows:
            send("oP2", cross, rows, self.partner)
        if self.core is not None:
            send("c00", 0, rows, self.core)

    def step1(self):
        half, rows = self.rows // 2, self.rows
        self.wait("oA+")
        self.go("fA+", -1, 0, 0, half, self.nxt)
        self.wait("oB-")
        self.go("fB-", 1, 0, half, rows, self.prv)

    def step2(self):
        cross, ch = self.cross, self.cross // 2
        self.wait("oPA")
        self.go("pA+", 0, 1, 0, ch, self.nxt)
        self.wait("oPB")
        self.go("pB-", 0, 1, ch, cross, self.prv)
        self.go("pB+", 0, 1, ch, cross, self.nxt)
        self.go("pA-", 0, 1, 0, ch, self.prv)
        if cross < self.rows:
            self.wait("oP2")
        if self.core is not None:
            self.go("c01", 0, 1, 0, self.rows, self.core)

    def step3(self):
        rows, cross = self.rows, self.cross
        self.wait("oB+", "oA-")
        if cross < rows:
            self.go("y-", -1, 0, cross, rows, self.partner)
            self.go("y+", 1, 0, cross, rows, self.partner)
        if self.core is not None:
            self.go("c-0", -1, 0, 0, rows, self.core)
            self.go("c+0", 1, 0, 0, rows, self.core)

    def step4(self):
        rows, cross = self.rows, self.cross
        self.wait("fA+", "fB-")
        if cross < rows:
            self.go("y2", 2, 0, cross, rows, self.partner)
        if self.core is not None:
            self.go("c20", 2, 0, 0, rows, self.core)

    def step5(self):
        cross, ch = self.cross, self.cross // 2
        self.wait("pA+")
        self.go("qA+", -1, 1, 0, ch, self.nxt)
        self.wait("pB-")
        self.go("qB-", 1, 1, ch, cross, self.prv)

    def step6(self):
        self.wait("pB+", "pA-")
        if self.cross < self.rows:
            self.wait("y-", "y+")
        if self.core is not None:
            self.go("c-1", -1, 1, 0, self.rows, self.core)
            self.go("c+1", 1, 1, 0, self.rows, self.core)

    def step7(self):
        self.wait("qA+", "qB-")
        if self.cross < self.rows:
            self.wait("y2")
        if self.core is not None:
            self.go("c21", 2, 1, 0, self.rows, self.core)


def dp_of(z, yh, c):
    return lax.rem(z + 4, 4) * 4 + yh * 2 + c


def t_of(x, yl):
    return lax.rem(x + 4, 4) * 2 + yl


def kernel(
    s_ref, c_ref, w_ref, m1_ref, m2_ref, x_ref, gain_ref, wo_ref, cos_ref, sin_ref,
    upd_ref, out_ref,
    sv, ld, sb, cb, wv, m1v, m2v, wb, nb, stage, acc, kv, att, woo, wop, part, r1, r2, fp,
    send, recv, send2, recv2, local,
):
    d, t, z, yh, c, x, yl = place()
    core = (d + 1 - 2 * c, t)
    yhp = (dp_of(z, 1 - yh, c), t)
    ylp = (d, t_of(x, 1 - yl))
    far_y = lax.rem(2 * yh + yl + 3 + 2 * yl, 4)
    yfar = (dp_of(z, far_y // 2, c), t_of(x, lax.rem(far_y, 2)))
    xn, xp = (d, t_of(x + 1, yl)), (d, t_of(x - 1, yl))
    zn, zp = (dp_of(z + 1, yh, c), t), (dp_of(z - 1, yh, c), t)
    others = [lax.rem(d + j, N_DP) for j in range(1, N_DP)]
    mine = mo(yl * HALF, HALF)
    theirs = mo((1 - yl) * HALF, HALF)

    def spread(e):
        return sv.at[:, pl.ds(mo(e * ROWS, ROWS), ROWS)]

    landing = ld.at[pl.ds(mo(d * SUB, SUB), SUB), :]

    def fetch(i):
        return pltpu.make_async_copy(
            x_ref.at[pl.ds(mo(i * NR, NR), NR), :], stage.at[lax.rem(i, 2)],
            local.at[lax.rem(i, 2)],
        )

    own_c = pltpu.make_async_copy(c_ref, cb.at[d], local.at[2])
    load_s = pltpu.make_async_copy(s_ref.at[pl.ds(mo(t * SUB, SUB), SUB), :], sv, local.at[3])
    own_s = pltpu.make_async_copy(spread(d), landing, local.at[4])
    state = [
        pltpu.make_async_copy(src, dst, local.at[5 + i])
        for i, (src, dst) in enumerate(((w_ref, wv), (m1_ref, m1v), (m2_ref, m2v)))
    ]
    out_w = pltpu.make_async_copy(wo_ref.at[:, pl.ds(mine, HALF)], woo, local.at[8])
    split = [
        pltpu.make_async_copy(ld.at[:, pl.ds(h * HR, HR)], sb.at[h, t], local.at[9 + h])
        for h in range(2)
    ]
    load_s.start()
    own_c.start()
    fetch(0).start()
    greet([(e, t) for e in others] + [xn, xp, ylp, yfar])
    load_s.wait()

    cps = Copies(send, recv)

    def dp_index(rr, p):
        return dp_of(z + rr, yh + p * (1 - 2 * yh), c)

    def t_index(rr, p):
        return t_of(x + rr, yl + p * (1 - 2 * yl))

    cot = Gather(("c",), cps, cb, dp_index, TOK, CROSS_C, zn, zp, yhp, core)
    sta = [
        Gather(("s", h), cps, sb.at[h], t_index, N_DP * SUB, CROSS_S, xn, xp, ylp)
        for h in range(2)
    ]
    gat = [
        Gather(("w", h), cps, wb.at[h], dp_index, HR, CROSS_W, zn, zp, yhp, core)
        for h in range(2)
    ]

    def norm(i, carry):
        @pl.when(i + 1 < LEN // NR)
        def _():
            fetch(i + 1).start()

        fetch(i).wait()
        slot = lax.rem(i, 2)

        def rows16(k, carry):
            r = pl.ds(mo(k * 16, 16), 16)
            ro = pl.ds(mo(i * NR + k * 16, 16), 16)
            tot = jnp.zeros((16, ROWS), F32)
            for j in range(N_DP):
                v = stage[slot, r, j * ROWS : (j + 1) * ROWS].astype(F32)
                tot = tot + v * v
            scale = lax.rsqrt(jnp.sum(tot, axis=1, keepdims=True) * (1.0 / D) + norm_eps)
            for j in range(N_DP):
                v = stage[slot, r, j * ROWS : (j + 1) * ROWS].astype(F32)
                gj = gain_ref[:, j * ROWS : (j + 1) * ROWS]
                nb[j, ro, :] = (v * scale * gj).astype(BF)
            return carry

        lax.fori_loop(0, NR // 16, rows16, 0)
        return carry

    def term(h, tb):
        cc = cb[:, pl.ds(mo(tb * SUB, SUB), SUB), :].reshape(N_DP * SUB, SLICE)
        return lax.dot_general(
            sb[h, tb], cc, (((0,), (0,)), ((), ())), preferred_element_type=F32
        )

    def gradient(h):
        rows = pl.ds(h * HR, HR)
        upd_ref[rows, :] = term(h, t)

        def one(i, carry):
            upd_ref[rows, :] += term(h, t_of(x + i // 2, lax.rem(yl + i, 2)))
            return carry

        lax.fori_loop(1, N_T, one, 0)

        def adam(i, carry):
            r = pl.ds(mo(h * HR + i * 32, 32), 32)
            grad = upd_ref[r, :]
            moment = beta_one * m1v[r, :] + (1.0 - beta_one) * grad
            second = beta_two * m2v[r, :] + (1.0 - beta_two) * grad * grad
            upd = moment / bias_one / (jnp.sqrt(second / bias_two) + adam_eps)
            upd_ref[r, :] = upd
            wb[h, d, pl.ds(mo(i * 32, 32), 32), :] = (wv[r, :] - learn_rate * upd).astype(BF)
            return carry

        lax.fori_loop(0, HR // 32, adam, 0)

    def project(h, rr, plane):
        e = dp_of(z + rr, yh + plane * (1 - 2 * yh), 0)
        hc = slice(h * HR, (h + 1) * HR)
        return jnp.dot(nb[e, :, hc], wb[h, e], preferred_element_type=F32) + jnp.dot(
            nb[e + 1, :, hc], wb[h, e + 1], preferred_element_type=F32
        )

    def project_ring(h, plane):
        def one(i, carry):
            acc[...] += project(h, i, plane)
            return carry

        lax.fori_loop(1, 4, one, 0)

    def here(h, *names):
        cps.arrived(*[("w", h) + (n,) for n in names])

    NN = LEN // NR
    for j, e in enumerate(others):
        cps.start(("a", j), spread(e), landing, (e, t))
    own_s.start()
    cot.begin(c_ref)
    for cp in state:
        cp.start()
    lax.fori_loop(0, 7, norm, 0)
    cps.arrived(*[("a", j) for j in range(N_DP - 1)])
    own_s.wait()
    for cp in split:
        cp.start()
    split[0].wait()
    sta[0].begin()
    cot.step1()
    sta[0].step1()
    cot.step2()
    sta[0].step2()
    sta[0].step3()
    cot.step3()
    sta[0].step4()
    cot.step4()
    sta[0].step5()
    split[1].wait()
    sta[1].begin()
    cot.step5()
    lax.fori_loop(7, NN, norm, 0)
    sta[0].step6()
    cot.step6()
    cot.step7()
    sta[0].step7()
    own_c.wait()
    for cp in state:
        cp.wait()
    cps.arrived(*[("c", n) for n in ("c00", "c01", "c-0", "c+0", "c20", "c-1", "c+1", "c21")])
    gradient(0)
    gat[0].begin()
    NP = QW // 8

    def weights(k):
        for i, peer in enumerate((ylp, yfar)):
            rows = pl.ds(mo((2 * c + i) * (QW // 4) + k * NP, NP), NP)
            cps.start(("o", i, k), wo_ref.at[rows, pl.ds(theirs, HALF)], wop.at[rows, :], peer)

    weights(0)
    sta[1].step1()
    sta[1].step2()
    out_w.start()
    gat[0].step1()
    gat[0].step2()
    sta[1].step3()
    sta[1].step4()
    gat[0].step3()
    sta[1].step5()
    here(0, "c00")
    acc[...] = project(0, 0, 0)
    gat[0].step4()
    sta[1].step6()
    gat[0].step5()
    sta[1].step7()
    gradient(1)
    gat[1].begin()
    weights(1)
    here(0, "c01")
    acc[...] += project(0, 0, 1)
    here(0, "c-0", "c+0", "c20")
    project_ring(0, 0)
    gat[0].step6()
    gat[0].step7()
    gat[1].step1()
    gat[1].step2()
    here(0, "c-1", "c+1", "c21")
    project_ring(0, 1)
    gat[1].step3()
    here(1, "c00", "c01")
    acc[...] += project(1, 0, 0)
    gat[1].step4()
    acc[...] += project(1, 0, 1)
    gat[1].step5()
    cps.arrived(*[("o", i, k) for i in range(2) for k in range(2)])
    wc = pl.ds(mo(c * (QW // 2), QW // 2), QW // 2)
    cps.start("oc", wop.at[wc, :], wop.at[wc, :], core)
    gat[1].step6()
    here(1, "c-0", "c+0", "c20")
    project_ring(1, 0)
    gat[1].step7()
    here(1, "c-1", "c+1", "c21")
    project_ring(1, 1)

    def rope(u, rows):
        return u * cos_ref[rows, :] + pltpu.roll(u, HD // 2, 1) * sin_ref[rows, :]

    XB = LEN // 4
    HC = CW // 2
    whole = pl.ds(0, LEN)
    kv[0] = rope(acc[:, QW : QW + HD], whole).astype(BF)
    kv[1] = acc[:, QW + HD :].astype(BF)

    def rows_of(xx):
        return pl.ds(mo(lax.rem(xx + 4, 4) * XB, XB), XB)

    def attend(xx):
        rows = rows_of(xx)
        q = jnp.concatenate(
            [
                (rope(acc[rows, h * HD : (h + 1) * HD], rows) * (HD**-0.5)).astype(BF)
                for h in range(QH)
            ],
            axis=0,
        )
        s = lax.dot_general(
            q, kv[0], (((1,), (1,)), ((), ())), preferred_element_type=F32
        )
        qi = lax.broadcasted_iota(jnp.int32, (QH * XB, LEN), 0) % XB
        ki = lax.broadcasted_iota(jnp.int32, (QH * XB, LEN), 1)
        s = jnp.where(qi + lax.rem(xx + 4, 4) * XB >= ki, s, -jnp.inf)
        e = jnp.exp(s - jnp.max(s, axis=1, keepdims=True))
        a = (e * (1.0 / jnp.sum(e, axis=1, keepdims=True))).astype(BF)
        o = jnp.dot(a, kv[1], preferred_element_type=F32).astype(BF)
        for h in range(QH):
            att[0, rows, h * HD : (h + 1) * HD] = o[h * XB : (h + 1) * XB]

    def share(i, xx):
        rows = rows_of(xx)
        cps.start(("t", i), att.at[0, rows, :], att.at[1, rows, :], ylp)

    def cols_of(k, w=CW, off=0):
        return pl.ds(mo(k * CW + off, HC), w)

    def remote(src, dst, i, peer):
        return pltpu.make_async_remote_copy(
            src_ref=src, dst_ref=dst, send_sem=send2.at[i], recv_sem=recv2.at[i],
            device_id=peer, device_id_type=MESH,
        )

    def far(k):
        hc = pl.ds(mo(k * HC, HC), HC)
        return (
            remote(part.at[rows_of(x + 2), cols_of(k, HC)], r1.at[0, :, hc], k, xn),
            remote(part.at[rows_of(x + 2), cols_of(k, HC, HC)], r1.at[1, :, hc], CHUNKS + k, xp),
        )

    def near(k):
        return (
            remote(part.at[rows_of(x + 1), cols_of(k)], r2.at[0, :, cols_of(k)], 2 * CHUNKS + k, xn),
            remote(part.at[rows_of(x - 1), cols_of(k)], r2.at[1, :, cols_of(k)], 3 * CHUNKS + k, xp),
        )

    def last(k):
        oc = pl.ds(mo(mine + k * CW, CW), CW)
        return remote(fp.at[:, cols_of(k)], out_ref.at[:, oc], 4 * CHUNKS + k, ylp)

    def produce(xx, then=None):
        rows = rows_of(xx)

        def chunk(k, carry):
            def tile(j, carry):
                cc = pl.ds(mo(k * CW + j * 256, 256), 256)
                part[rows, cc] = (
                    jnp.dot(att[0, rows, :], woo[:, cc], preferred_element_type=F32)
                    + jnp.dot(att[1, rows, :], wop[:, cc], preferred_element_type=F32)
                ).astype(BF)
                return carry

            lax.fori_loop(0, CW // 256, tile, 0)
            if then is not None:
                then(k)
            return carry

        lax.fori_loop(0, CHUNKS, chunk, 0)

    def send_far(k):
        for cp in far(k):
            cp.start()

    def forward(k, carry):
        hc = pl.ds(mo(k * HC, HC), HC)
        up, down = far(k)
        to_next, to_prev = near(k)
        for i, (cp, nx, rows, cc) in enumerate(
            (
                (up, to_next, rows_of(x + 1), cols_of(k, HC)),
                (down, to_prev, rows_of(x - 1), cols_of(k, HC, HC)),
            )
        ):
            cp.wait_recv()
            part[rows, cc] = (part[rows, cc].astype(F32) + r1[i, :, hc].astype(F32)).astype(BF)
            nx.start()
        return carry

    def finish(k, carry):
        to_next, to_prev = near(k)
        to_next.wait_recv()
        to_prev.wait_recv()
        SR = LEN // N_T

        def total(half):
            rows = pl.ds(mo(x * XB + half * SR, SR), SR)
            rr = pl.ds(mo(half * SR, SR), SR)
            cc = cols_of(k)
            return (
                part[rows, cc].astype(F32)
                + r2[0, rr, cc].astype(F32)
                + r2[1, rr, cc].astype(F32)
            ).astype(BF)

        fp[:, cols_of(k)] = total(1 - yl)
        last(k).start()
        out_ref[:, pl.ds(mo(mine + k * CW, CW), CW)] = total(yl)
        return carry

    def close(k, carry):
        for cp in far(k) + near(k):
            cp.wait_send()
        last(k).wait()
        return carry

    attend(x + 2)
    share(0, x + 2)
    attend(x + 1)
    share(1, x + 1)
    out_w.wait()
    cps.arrived("oc", ("t", 0))
    produce(x + 2, send_far)
    attend(x - 1)
    share(2, x - 1)
    attend(x)
    share(3, x)
    cps.arrived(("t", 1))
    produce(x + 1)
    cps.arrived(("t", 2))
    produce(x - 1)
    lax.fori_loop(0, CHUNKS, forward, 0)
    cps.arrived(("t", 3))
    produce(x)
    lax.fori_loop(0, CHUNKS, finish, 0)
    lax.fori_loop(0, CHUNKS, close, 0)
    cps.drain()


CROSS_C = 160
CROSS_S = N_DP * SUB
CROSS_W = 224


def tables():
    half = HD // 2
    exponent = np.arange(half, dtype=np.float32) * np.float32(2.0 / HD)
    inverse = np.power(np.float64(rope_base), -exponent.astype(np.float64)).astype(np.float32)
    angles = np.arange(LEN, dtype=np.float32)[:, None] * inverse[None, :]
    cos = np.cos(angles.astype(np.float64)).astype(np.float32)
    sin = np.sin(angles.astype(np.float64)).astype(np.float32)
    return np.concatenate([cos, cos], 1), np.concatenate([-sin, sin], 1)


ANY = pl.BlockSpec(memory_space=pl.ANY)
VM = pl.BlockSpec(memory_space=pltpu.VMEM)


def step(*args, name="adam_prefill"):
    dma = pltpu.SemaphoreType.DMA
    cos, sin = tables()
    return pl.pallas_call(
        kernel,
        name=name,
        out_shape=(
            jax.ShapeDtypeStruct((ROWS, SLICE), F32),
            jax.ShapeDtypeStruct((LEN // N_T, D), BF),
        ),
        in_specs=[ANY] * 6 + [VM, ANY, VM, VM],
        out_specs=(VM, VM),
        scratch_shapes=[
            pltpu.VMEM((SUB, D), BF),
            pltpu.VMEM((N_DP * SUB, ROWS), BF),
            pltpu.VMEM((2, N_T, N_DP * SUB, HR), BF),
            pltpu.VMEM((N_DP, TOK, SLICE), BF),
            pltpu.VMEM((ROWS, SLICE), F32),
            pltpu.VMEM((ROWS, SLICE), F32),
            pltpu.VMEM((ROWS, SLICE), F32),
            pltpu.VMEM((2, N_DP, HR, SLICE), BF),
            pltpu.VMEM((N_DP, LEN, ROWS), BF),
            pltpu.VMEM((2, NR, D), BF),
            pltpu.VMEM((LEN, SLICE), F32),
            pltpu.VMEM((2, LEN, HD), BF),
            pltpu.VMEM((2, LEN, QW), BF),
            pltpu.VMEM((QW, HALF), BF),
            pltpu.VMEM((QW, HALF), BF),
            pltpu.VMEM((LEN, HALF), BF),
            pltpu.VMEM((2, LEN // 4, HALF // 2), BF),
            pltpu.VMEM((2, LEN // 4, HALF), BF),
            pltpu.VMEM((LEN // N_T, HALF), BF),
            dma((N_COPIES,)),
            dma((N_COPIES,)),
            dma((5 * CHUNKS,)),
            dma((5 * CHUNKS,)),
            dma((11,)),
        ],
        compiler_params=pltpu.CompilerParams(
            collective_id=1, has_side_effects=True, vmem_limit_bytes=67043328
        ),
    )(*args[:6], args[6].reshape(1, D), args[7], jnp.asarray(cos), jnp.asarray(sin))


def body(
    train_states, qkv_cotangent, w_master, moment_one, moment_two, prompt_states, norm_gain, w_out
):
    return step(
        train_states, qkv_cotangent, w_master, moment_one, moment_two,
        prompt_states, norm_gain, w_out,
    )


def solution(mesh):
    placed = (
        P("dp", None),
        P("dp", "tensor"),
        P("dp", "tensor"),
        P("dp", "tensor"),
        P("dp", "tensor"),
        P("dp", None),
        P(),
        P("tensor", None),
    )
    return jax.shard_map(
        body,
        mesh=mesh,
        in_specs=placed,
        out_specs=(P("dp", "tensor"), P(("dp", "tensor"), None)),
        check_vma=False,
    )
```

```python
import jax
import jax.numpy as jnp
import numpy as np
from jax import lax
from jax.experimental import pallas as pl
from jax.experimental.pallas import tpu as pltpu
from jax.sharding import PartitionSpec as P

HD = 128
QH = 4
LEN = 512
D = 8192
N_DP = 16
N_T = 8
SLICE = (QH + 2) * HD
QW = QH * HD
ROWS = D // N_DP
TOK = 256
SUB = TOK // N_T
HALF = D // 2
CHUNKS = 4
CW = HALF // CHUNKS
HR = ROWS // 2
NR = 32
N_COPIES = 200

beta_one = 0.9
beta_two = 0.95
bias_one = 1.0 - 0.9**8
bias_two = 1.0 - 0.95**8
learn_rate = 0.002
adam_eps = 1e-08
norm_eps = 1e-05
rope_base = 500000.0

MESH = pl.DeviceIdType.MESH
BF = jnp.bfloat16
F32 = jnp.float32


def place():
    d = lax.axis_index("dp")
    t = lax.axis_index("tensor")
    return d, t, d // 4, (d // 2) % 2, d % 2, t // 2, t % 2


def mo(v, m):
    return pl.multiple_of(v, m)


def greet(peers):
    barrier = pltpu.get_barrier_semaphore()
    for peer in peers:
        pl.semaphore_signal(barrier, inc=1, device_id=peer, device_id_type=MESH)
    pl.semaphore_wait(barrier, len(peers))


class Copies:
    def __init__(self, send, recv):
        self.send, self.recv, self.made, self.used = send, recv, {}, 0

    def start(self, name, src, dst, peer):
        cp = pltpu.make_async_remote_copy(
            src_ref=src,
            dst_ref=dst,
            send_sem=self.send.at[self.used],
            recv_sem=self.recv.at[self.used],
            device_id=peer,
            device_id_type=MESH,
        )
        self.used += 1
        self.made[name] = cp
        cp.start()

    def arrived(self, *names):
        for name in names:
            self.made[name].wait_recv()

    def drain(self):
        for cp in self.made.values():
            cp.wait_send()


class Gather:
    def __init__(
        self, tag, cps, buf, index, rows, cross, nxt, prv, partner, core=None
    ):
        self.tag, self.cps, self.buf, self.index = tag, cps, buf, index
        self.rows, self.cross = rows, cross
        self.nxt, self.prv, self.partner, self.core = nxt, prv, partner, core

    def piece(self, rr, plane, lo, hi):
        return self.buf.at[self.index(rr, plane), pl.ds(lo, hi - lo), :]

    def go(self, name, rr, plane, lo, hi, peer, src=None):
        dst = self.piece(rr, plane, lo, hi)
        if src is None:
            src = dst
        self.cps.start(self.tag + (name,), src, dst, peer)

    def wait(self, *names):
        self.cps.arrived(*[self.tag + (name,) for name in names])

    def begin(self, own=None):
        rows, cross = self.rows, self.cross
        half, ch = rows // 2, self.cross // 2

        def src(lo, hi):
            if own is None:
                return None
            return own.at[pl.ds(lo, hi - lo), :]

        def send(name, lo, hi, peer):
            self.go(name, 0, 0, lo, hi, peer, src(lo, hi))

        send("oA+", 0, half, self.nxt)
        send("oB-", half, rows, self.prv)
        send("oPA", 0, ch, self.partner)
        send("oPB", ch, cross, self.partner)
        send("oB+", half, rows, self.nxt)
        send("oA-", 0, half, self.prv)
        if cross < rows:
            send("oP2", cross, rows, self.partner)
        if self.core is not None:
            send("c00", 0, rows, self.core)

    def step1(self):
        half, rows = self.rows // 2, self.rows
        self.wait("oA+")
        self.go("fA+", -1, 0, 0, half, self.nxt)
        self.wait("oB-")
        self.go("fB-", 1, 0, half, rows, self.prv)

    def step2(self):
        cross, ch = self.cross, self.cross // 2
        self.wait("oPA")
        self.go("pA+", 0, 1, 0, ch, self.nxt)
        self.wait("oPB")
        self.go("pB-", 0, 1, ch, cross, self.prv)
        self.go("pB+", 0, 1, ch, cross, self.nxt)
        self.go("pA-", 0, 1, 0, ch, self.prv)
        if cross < self.rows:
            self.wait("oP2")
        if self.core is not None:
            self.go("c01", 0, 1, 0, self.rows, self.core)

    def step3(self):
        rows, cross = self.rows, self.cross
        self.wait("oB+", "oA-")
        if cross < rows:
            self.go("y-", -1, 0, cross, rows, self.partner)
            self.go("y+", 1, 0, cross, rows, self.partner)
        if self.core is not None:
            self.go("c-0", -1, 0, 0, rows, self.core)
            self.go("c+0", 1, 0, 0, rows, self.core)

    def step4(self):
        rows, cross = self.rows, self.cross
        self.wait("fA+", "fB-")
        if cross < rows:
            self.go("y2", 2, 0, cross, rows, self.partner)
        if self.core is not None:
            self.go("c20", 2, 0, 0, rows, self.core)

    def step5(self):
        cross, ch = self.cross, self.cross // 2
        self.wait("pA+")
        self.go("qA+", -1, 1, 0, ch, self.nxt)
        self.wait("pB-")
        self.go("qB-", 1, 1, ch, cross, self.prv)

    def step6(self):
        self.wait("pB+", "pA-")
        if self.cross < self.rows:
            self.wait("y-", "y+")
        if self.core is not None:
            self.go("c-1", -1, 1, 0, self.rows, self.core)
            self.go("c+1", 1, 1, 0, self.rows, self.core)

    def step7(self):
        self.wait("qA+", "qB-")
        if self.cross < self.rows:
            self.wait("y2")
        if self.core is not None:
            self.go("c21", 2, 1, 0, self.rows, self.core)


def dp_of(z, yh, c):
    return lax.rem(z + 4, 4) * 4 + yh * 2 + c


def t_of(x, yl):
    return lax.rem(x + 4, 4) * 2 + yl


def kernel(
    s_ref, c_ref, w_ref, m1_ref, m2_ref, x_ref, gain_ref, wo_ref, cos_ref, sin_ref,
    upd_ref, out_ref,
    sv, ld, sb, cb, wv, m1v, m2v, wb, nb, stage, acc, kv, att, woo, wop, part, r1, r2, fp,
    send, recv, send2, recv2, local,
):
    d, t, z, yh, c, x, yl = place()
    core = (d + 1 - 2 * c, t)
    yhp = (dp_of(z, 1 - yh, c), t)
    ylp = (d, t_of(x, 1 - yl))
    far_y = lax.rem(2 * yh + yl + 3 + 2 * yl, 4)
    yfar = (dp_of(z, far_y // 2, c), t_of(x, lax.rem(far_y, 2)))
    xn, xp = (d, t_of(x + 1, yl)), (d, t_of(x - 1, yl))
    zn, zp = (dp_of(z + 1, yh, c), t), (dp_of(z - 1, yh, c), t)
    others = [lax.rem(d + j, N_DP) for j in range(1, N_DP)]
    mine = mo(yl * HALF, HALF)
    theirs = mo((1 - yl) * HALF, HALF)

    def spread(e):
        return sv.at[:, pl.ds(mo(e * ROWS, ROWS), ROWS)]

    landing = ld.at[pl.ds(mo(d * SUB, SUB), SUB), :]

    def fetch(i):
        return pltpu.make_async_copy(
            x_ref.at[pl.ds(mo(i * NR, NR), NR), :], stage.at[lax.rem(i, 2)],
            local.at[lax.rem(i, 2)],
        )

    own_c = pltpu.make_async_copy(c_ref, cb.at[d], local.at[2])
    load_s = pltpu.make_async_copy(s_ref.at[pl.ds(mo(t * SUB, SUB), SUB), :], sv, local.at[3])
    own_s = pltpu.make_async_copy(spread(d), landing, local.at[4])
    state = [
        pltpu.make_async_copy(src, dst, local.at[5 + i])
        for i, (src, dst) in enumerate(((w_ref, wv), (m1_ref, m1v), (m2_ref, m2v)))
    ]
    out_w = pltpu.make_async_copy(wo_ref.at[:, pl.ds(mine, HALF)], woo, local.at[8])
    split = [
        pltpu.make_async_copy(ld.at[:, pl.ds(h * HR, HR)], sb.at[h, t], local.at[9 + h])
        for h in range(2)
    ]
    load_s.start()
    own_c.start()
    fetch(0).start()
    greet([(e, t) for e in others] + [xn, xp, ylp, yfar])
    load_s.wait()

    cps = Copies(send, recv)

    def dp_index(rr, p):
        return dp_of(z + rr, yh + p * (1 - 2 * yh), c)

    def t_index(rr, p):
        return t_of(x + rr, yl + p * (1 - 2 * yl))

    cot = Gather(("c",), cps, cb, dp_index, TOK, CROSS_C, zn, zp, yhp, core)
    sta = [
        Gather(("s", h), cps, sb.at[h], t_index, N_DP * SUB, CROSS_S, xn, xp, ylp)
        for h in range(2)
    ]
    gat = [
        Gather(("w", h), cps, wb.at[h], dp_index, HR, CROSS_W, zn, zp, yhp, core)
        for h in range(2)
    ]

    def norm(i, carry):
        @pl.when(i + 1 < LEN // NR)
        def _():
            fetch(i + 1).start()

        fetch(i).wait()
        slot = lax.rem(i, 2)

        def rows16(k, carry):
            r = pl.ds(mo(k * 16, 16), 16)
            ro = pl.ds(mo(i * NR + k * 16, 16), 16)
            tot = jnp.zeros((16, ROWS), F32)
            for j in range(N_DP):
                v = stage[slot, r, j * ROWS : (j + 1) * ROWS].astype(F32)
                tot = tot + v * v
            scale = lax.rsqrt(jnp.sum(tot, axis=1, keepdims=True) * (1.0 / D) + norm_eps)
            for j in range(N_DP):
                v = stage[slot, r, j * ROWS : (j + 1) * ROWS].astype(F32)
                gj = gain_ref[:, j * ROWS : (j + 1) * ROWS]
                nb[j, ro, :] = (v * scale * gj).astype(BF)
            return carry

        lax.fori_loop(0, NR // 16, rows16, 0)
        return carry

    def term(h, tb):
        cc = cb[:, pl.ds(mo(tb * SUB, SUB), SUB), :].reshape(N_DP * SUB, SLICE)
        return lax.dot_general(
            sb[h, tb], cc, (((0,), (0,)), ((), ())), preferred_element_type=F32
        )

    def gradient(h):
        rows = pl.ds(h * HR, HR)
        upd_ref[rows, :] = term(h, t)

        def one(i, carry):
            upd_ref[rows, :] += term(h, t_of(x + i // 2, lax.rem(yl + i, 2)))
            return carry

        lax.fori_loop(1, N_T, one, 0)

        def adam(i, carry):
            r = pl.ds(mo(h * HR + i * 32, 32), 32)
            grad = upd_ref[r, :]
            moment = beta_one * m1v[r, :] + (1.0 - beta_one) * grad
            second = beta_two * m2v[r, :] + (1.0 - beta_two) * grad * grad
            upd = moment / bias_one / (jnp.sqrt(second / bias_two) + adam_eps)
            upd_ref[r, :] = upd
            wb[h, d, pl.ds(mo(i * 32, 32), 32), :] = (wv[r, :] - learn_rate * upd).astype(BF)
            return carry

        lax.fori_loop(0, HR // 32, adam, 0)

    def project(h, rr, plane):
        e = dp_of(z + rr, yh + plane * (1 - 2 * yh), 0)
        hc = slice(h * HR, (h + 1) * HR)
        return jnp.dot(nb[e, :, hc], wb[h, e], preferred_element_type=F32) + jnp.dot(
            nb[e + 1, :, hc], wb[h, e + 1], preferred_element_type=F32
        )

    def project_ring(h, plane):
        def one(i, carry):
            acc[...] += project(h, i, plane)
            return carry

        lax.fori_loop(1, 4, one, 0)

    def here(h, *names):
        cps.arrived(*[("w", h) + (n,) for n in names])

    NN = LEN // NR
    for j, e in enumerate(others):
        cps.start(("a", j), spread(e), landing, (e, t))
    own_s.start()
    cot.begin(c_ref)
    for cp in state:
        cp.start()
    lax.fori_loop(0, 7, norm, 0)
    cps.arrived(*[("a", j) for j in range(N_DP - 1)])
    own_s.wait()
    for cp in split:
        cp.start()
    split[0].wait()
    sta[0].begin()
    cot.step1()
    sta[0].step1()
    cot.step2()
    sta[0].step2()
    sta[0].step3()
    cot.step3()
    sta[0].step4()
    cot.step4()
    sta[0].step5()
    split[1].wait()
    sta[1].begin()
    cot.step5()
    lax.fori_loop(7, NN, norm, 0)
    sta[0].step6()
    cot.step6()
    cot.step7()
    sta[0].step7()
    own_c.wait()
    for cp in state:
        cp.wait()
    cps.arrived(*[("c", n) for n in ("c00", "c01", "c-0", "c+0", "c20", "c-1", "c+1", "c21")])
    gradient(0)
    gat[0].begin()
    NP = QW // 8

    def weights(k):
        for i, peer in enumerate((ylp, yfar)):
            rows = pl.ds(mo((2 * c + i) * (QW // 4) + k * NP, NP), NP)
            cps.start(("o", i, k), wo_ref.at[rows, pl.ds(theirs, HALF)], wop.at[rows, :], peer)

    weights(0)
    sta[1].step1()
    sta[1].step2()
    out_w.start()
    gat[0].step1()
    gat[0].step2()
    sta[1].step3()
    sta[1].step4()
    gat[0].step3()
    sta[1].step5()
    here(0, "c00")
    acc[...] = project(0, 0, 0)
    gat[0].step4()
    sta[1].step6()
    gat[0].step5()
    sta[1].step7()
    gradient(1)
    gat[1].begin()
    weights(1)
    here(0, "c01")
    acc[...] += project(0, 0, 1)
    here(0, "c-0", "c+0", "c20")
    project_ring(0, 0)
    gat[0].step6()
    gat[0].step7()
    gat[1].step1()
    gat[1].step2()
    here(0, "c-1", "c+1", "c21")
    project_ring(0, 1)
    gat[1].step3()
    here(1, "c00", "c01")
    acc[...] += project(1, 0, 0)
    gat[1].step4()
    acc[...] += project(1, 0, 1)
    gat[1].step5()
    cps.arrived(*[("o", i, k) for i in range(2) for k in range(2)])
    wc = pl.ds(mo(c * (QW // 2), QW // 2), QW // 2)
    cps.start("oc", wop.at[wc, :], wop.at[wc, :], core)
    gat[1].step6()
    here(1, "c-0", "c+0", "c20")
    project_ring(1, 0)
    gat[1].step7()
    here(1, "c-1", "c+1", "c21")
    project_ring(1, 1)

    def rope(u, rows):
        return u * cos_ref[rows, :] + pltpu.roll(u, HD // 2, 1) * sin_ref[rows, :]

    XB = LEN // 4
    HC = CW // 2
    whole = pl.ds(0, LEN)
    kv[0] = rope(acc[:, QW : QW + HD], whole).astype(BF)
    kv[1] = acc[:, QW + HD :].astype(BF)

    def rows_of(xx):
        return pl.ds(mo(lax.rem(xx + 4, 4) * XB, XB), XB)

    def attend(xx):
        rows = rows_of(xx)
        q = jnp.concatenate(
            [
                (rope(acc[rows, h * HD : (h + 1) * HD], rows) * (HD**-0.5)).astype(BF)
                for h in range(QH)
            ],
            axis=0,
        )
        s = lax.dot_general(
            q, kv[0], (((1,), (1,)), ((), ())), preferred_element_type=F32
        )
        qi = lax.broadcasted_iota(jnp.int32, (QH * XB, LEN), 0) % XB
        ki = lax.broadcasted_iota(jnp.int32, (QH * XB, LEN), 1)
        s = jnp.where(qi + lax.rem(xx + 4, 4) * XB >= ki, s, -jnp.inf)
        e = jnp.exp(s - jnp.max(s, axis=1, keepdims=True))
        a = (e * (1.0 / jnp.sum(e, axis=1, keepdims=True))).astype(BF)
        o = jnp.dot(a, kv[1], preferred_element_type=F32).astype(BF)
        for h in range(QH):
            att[0, rows, h * HD : (h + 1) * HD] = o[h * XB : (h + 1) * XB]

    def share(i, xx):
        rows = rows_of(xx)
        cps.start(("t", i), att.at[0, rows, :], att.at[1, rows, :], ylp)

    def cols_of(k, w=CW, off=0):
        return pl.ds(mo(k * CW + off, HC), w)

    def remote(src, dst, i, peer):
        return pltpu.make_async_remote_copy(
            src_ref=src, dst_ref=dst, send_sem=send2.at[i], recv_sem=recv2.at[i],
            device_id=peer, device_id_type=MESH,
        )

    def far(k):
        hc = pl.ds(mo(k * HC, HC), HC)
        return (
            remote(part.at[rows_of(x + 2), cols_of(k, HC)], r1.at[0, :, hc], k, xn),
            remote(part.at[rows_of(x + 2), cols_of(k, HC, HC)], r1.at[1, :, hc], CHUNKS + k, xp),
        )

    def near(k):
        return (
            remote(part.at[rows_of(x + 1), cols_of(k)], r2.at[0, :, cols_of(k)], 2 * CHUNKS + k, xn),
            remote(part.at[rows_of(x - 1), cols_of(k)], r2.at[1, :, cols_of(k)], 3 * CHUNKS + k, xp),
        )

    def last(k):
        oc = pl.ds(mo(mine + k * CW, CW), CW)
        return remote(fp.at[:, cols_of(k)], out_ref.at[:, oc], 4 * CHUNKS + k, ylp)

    def produce(xx, then=None):
        rows = rows_of(xx)

        def chunk(k, carry):
            def tile(j, carry):
                cc = pl.ds(mo(k * CW + j * 256, 256), 256)
                part[rows, cc] = (
                    jnp.dot(att[0, rows, :], woo[:, cc], preferred_element_type=F32)
                    + jnp.dot(att[1, rows, :], wop[:, cc], preferred_element_type=F32)
                ).astype(BF)
                return carry

            lax.fori_loop(0, CW // 256, tile, 0)
            if then is not None:
                then(k)
            return carry

        lax.fori_loop(0, CHUNKS, chunk, 0)

    def send_far(k):
        for cp in far(k):
            cp.start()

    def forward(k, carry):
        hc = pl.ds(mo(k * HC, HC), HC)
        up, down = far(k)
        to_next, to_prev = near(k)
        for i, (cp, nx, rows, cc) in enumerate(
            (
                (up, to_next, rows_of(x + 1), cols_of(k, HC)),
                (down, to_prev, rows_of(x - 1), cols_of(k, HC, HC)),
            )
        ):
            cp.wait_recv()
            part[rows, cc] = (part[rows, cc].astype(F32) + r1[i, :, hc].astype(F32)).astype(BF)
            nx.start()
        return carry

    def finish(k, carry):
        to_next, to_prev = near(k)
        to_next.wait_recv()
        to_prev.wait_recv()
        SR = LEN // N_T

        def total(half):
            rows = pl.ds(mo(x * XB + half * SR, SR), SR)
            rr = pl.ds(mo(half * SR, SR), SR)
            cc = cols_of(k)
            return (
                part[rows, cc].astype(F32)
                + r2[0, rr, cc].astype(F32)
                + r2[1, rr, cc].astype(F32)
            ).astype(BF)

        fp[:, cols_of(k)] = total(1 - yl)
        last(k).start()
        out_ref[:, pl.ds(mo(mine + k * CW, CW), CW)] = total(yl)
        return carry

    def close(k, carry):
        for cp in far(k) + near(k):
            cp.wait_send()
        last(k).wait()
        return carry

    attend(x + 2)
    share(0, x + 2)
    attend(x + 1)
    share(1, x + 1)
    out_w.wait()
    cps.arrived("oc", ("t", 0))
    produce(x + 2, send_far)
    attend(x - 1)
    share(2, x - 1)
    attend(x)
    share(3, x)
    cps.arrived(("t", 1))
    produce(x + 1)
    cps.arrived(("t", 2))
    produce(x - 1)
    lax.fori_loop(0, CHUNKS, forward, 0)
    cps.arrived(("t", 3))
    produce(x)
    lax.fori_loop(0, CHUNKS, finish, 0)
    lax.fori_loop(0, CHUNKS, close, 0)
    cps.drain()


CROSS_C = 192
CROSS_S = N_DP * SUB
CROSS_W = 224


def tables():
    half = HD // 2
    exponent = np.arange(half, dtype=np.float32) * np.float32(2.0 / HD)
    inverse = np.power(np.float64(rope_base), -exponent.astype(np.float64)).astype(np.float32)
    angles = np.arange(LEN, dtype=np.float32)[:, None] * inverse[None, :]
    cos = np.cos(angles.astype(np.float64)).astype(np.float32)
    sin = np.sin(angles.astype(np.float64)).astype(np.float32)
    return np.concatenate([cos, cos], 1), np.concatenate([-sin, sin], 1)


ANY = pl.BlockSpec(memory_space=pl.ANY)
VM = pl.BlockSpec(memory_space=pltpu.VMEM)


def step(*args, name="adam_prefill"):
    dma = pltpu.SemaphoreType.DMA
    cos, sin = tables()
    return pl.pallas_call(
        kernel,
        name=name,
        out_shape=(
            jax.ShapeDtypeStruct((ROWS, SLICE), F32),
            jax.ShapeDtypeStruct((LEN // N_T, D), BF),
        ),
        in_specs=[ANY] * 6 + [VM, ANY, VM, VM],
        out_specs=(VM, VM),
        scratch_shapes=[
            pltpu.VMEM((SUB, D), BF),
            pltpu.VMEM((N_DP * SUB, ROWS), BF),
            pltpu.VMEM((2, N_T, N_DP * SUB, HR), BF),
            pltpu.VMEM((N_DP, TOK, SLICE), BF),
            pltpu.VMEM((ROWS, SLICE), F32),
            pltpu.VMEM((ROWS, SLICE), F32),
            pltpu.VMEM((ROWS, SLICE), F32),
            pltpu.VMEM((2, N_DP, HR, SLICE), BF),
            pltpu.VMEM((N_DP, LEN, ROWS), BF),
            pltpu.VMEM((2, NR, D), BF),
            pltpu.VMEM((LEN, SLICE), F32),
            pltpu.VMEM((2, LEN, HD), BF),
            pltpu.VMEM((2, LEN, QW), BF),
            pltpu.VMEM((QW, HALF), BF),
            pltpu.VMEM((QW, HALF), BF),
            pltpu.VMEM((LEN, HALF), BF),
            pltpu.VMEM((2, LEN // 4, HALF // 2), BF),
            pltpu.VMEM((2, LEN // 4, HALF), BF),
            pltpu.VMEM((LEN // N_T, HALF), BF),
            dma((N_COPIES,)),
            dma((N_COPIES,)),
            dma((5 * CHUNKS,)),
            dma((5 * CHUNKS,)),
            dma((11,)),
        ],
        compiler_params=pltpu.CompilerParams(
            collective_id=1, has_side_effects=True, vmem_limit_bytes=67043328
        ),
    )(*args[:6], args[6].reshape(1, D), args[7], jnp.asarray(cos), jnp.asarray(sin))


def hand_over_kernel(u_ref, o_ref, u_out, o_out, sem):
    cps = [
        pltpu.make_async_copy(u_ref, u_out, sem.at[0]),
        pltpu.make_async_copy(o_ref, o_out, sem.at[1]),
    ]
    for cp in cps:
        cp.start()
    for cp in cps:
        cp.wait()


def hand_over(upd, out):
    return pl.pallas_call(
        hand_over_kernel,
        name="hand_over",
        out_shape=(
            jax.ShapeDtypeStruct(upd.shape, upd.dtype),
            jax.ShapeDtypeStruct(out.shape, out.dtype),
        ),
        in_specs=[VM, VM],
        out_specs=(ANY, ANY),
        scratch_shapes=[pltpu.SemaphoreType.DMA((2,))],
        compiler_params=pltpu.CompilerParams(vmem_limit_bytes=8 << 20),
    )(upd, out)


def body(
    train_states, qkv_cotangent, w_master, moment_one, moment_two, prompt_states, norm_gain, w_out
):
    return hand_over(
        *step(
            train_states, qkv_cotangent, w_master, moment_one, moment_two,
            prompt_states, norm_gain, w_out,
        )
    )


def solution(mesh):
    placed = (
        P("dp", None),
        P("dp", "tensor"),
        P("dp", "tensor"),
        P("dp", "tensor"),
        P("dp", "tensor"),
        P("dp", None),
        P(),
        P("tensor", None),
    )
    return jax.shard_map(
        body,
        mesh=mesh,
        in_specs=placed,
        out_specs=(P("dp", "tensor"), P(("dp", "tensor"), None)),
        check_vma=False,
    )
```
